32 devices in a mesh: weight: 2 (over x), ctx: 4 (over z), tensor: 4 (over y, core).
Axes of the slice: x: 2, y: 2, z: 4, core: 2. Of those that a mesh axis runs over, the one named last changes fastest.
Arguments:
- inputs: bfloat16 [2, 1024, 1024], P('weight', 'ctx'), may hold values from -40 to 40
- w_qkv: bfloat16 [1024, 3, 1024], P('weight', None, 'tensor'), may hold values from -4 to 4
- w_out: bfloat16 [1024, 1024], P('weight', 'tensor'), may hold values from -2 to 2
- w_up: bfloat16 [1024, 4096], P('weight', 'tensor'), may hold values from -0.1875 to 0.1875
- w_down: bfloat16 [1024, 4096], P('weight', 'tensor'), may hold values from -0.09375 to 0.09375
- head_bias: float32 [2, 1024], P(None, 'tensor'), may hold values from -3 to 3
- up_bias: float32 [4096], P('tensor'), may hold values from -3 to 3
- out_biases: float32 [2, 1024], replicated, may hold values from -3 to 3
- norm_gains: float32 [2, 1024], replicated, may hold values from 0.1 to 1.9
- norm_shifts: float32 [2, 1024], replicated, may hold values from -3 to 3
- cotangent: bfloat16 [2, 1024, 1024], P('weight', 'ctx'), may hold values from -6 to 6
Outputs:
- layer_out: bfloat16 [2, 1024, 1024], P('weight', 'ctx')
- grad_input: bfloat16 [2, 1024, 1024], P('weight', 'ctx')
- grad_w_qkv: float32 [1024, 3, 1024], P(('weight', 'ctx'), None, 'tensor')
- grad_w_out: float32 [1024, 1024], P(('weight', 'ctx'), 'tensor')
- grad_w_up: float32 [1024, 4096], P(('weight', 'ctx'), 'tensor')
- grad_w_down: float32 [1024, 4096], P(('weight', 'ctx'), 'tensor')
- grad_head_bias: float32 [2, 1024], P(None, 'tensor')
- grad_up_bias: float32 [4096], P('tensor')
- grad_out_biases: float32 [2, 1024], replicated
- grad_norm_gains: float32 [2, 1024], replicated
- grad_norm_shifts: float32 [2, 1024], replicated
The draws below stay inside these ranges and needn't reach their ends.
All inputs are finite; a program needn't handle non-finite values.
Results may differ from the reference program's by a relative error of at most 0.038.
Values may be sent and summed in bfloat16 or wider, within the bound.
No kernel may reach another device: no remote copies, remote signals or barrier semaphores. Data moves between devices by JAX's collectives and lax.ppermute only.
A program may use at most 128 MiB of HBM per device.

```python
import math
import jax
import jax.numpy as jnp
from jax import lax

D = 1024
H = 16
HD = 64
FF = 4096
SEQ = 1024
SEQS = 2


def draw_inputs(key, part):
    normal_key = jax.random.fold_in(key, 0)
    drawn = jax.random.truncated_normal(normal_key, -6.0, 6.0, (SEQS, SEQ, D), jnp.float32)
    return drawn.astype(jnp.bfloat16)


def draw_w_qkv(key, part):
    normal_key = jax.random.fold_in(key, 0)
    drawn = jax.random.truncated_normal(normal_key, -4.0, 4.0, (D, 3, D), jnp.float32) * (1.0 / math.sqrt(D))
    return drawn.astype(jnp.bfloat16)


def spiked(array, rng, source, target, blocks, factor):
    owner, partner = [(jnp.arange(array.shape[dim]) // (array.shape[dim] // blocks)).reshape([-1 if axis == dim else 1 for axis in range(array.ndim)]) for dim in (source, target)]
    chosen = jax.random.permutation(rng, blocks)[partner]
    strong = (owner == chosen) | (owner == (partner + blocks // 2) % blocks)
    return jnp.where(strong, factor * array, array)


def shard_levels(key, shape, cuts, smallest, top_value):
    factor_of, own = 1.0, jax.random.fold_in(key, 6)
    for position, parts in cuts:
        steps = jnp.exp(jax.random.uniform(jax.random.fold_in(own, position), (parts,), jnp.float32, smallest / len(cuts), top_value / len(cuts)))
        factor_of = factor_of * jnp.repeat(steps, shape[position] // parts).reshape([-1 if axis == position else 1 for axis in range(len(shape))])
    return factor_of


def gaussian(rng, extent, spread, most, cuts=(), dtype=jnp.bfloat16):
    array = jax.random.normal(rng, extent, jnp.float32) * spread
    if len(cuts) > 0:
        array = shard_levels(rng, extent, cuts, -0.22, 0.18) * array
    return jnp.clip(array, min=-most, max=most).astype(dtype)


def bell_draw_with(rng, extent, width, most, shards, heavy, held_as=jnp.bfloat16):
    values = width * jax.random.normal(rng, extent, jnp.float32)
    if shards:
        values = values * shard_levels(rng, extent, shards, -0.22, 0.18)
    return jnp.clip(spiked(values, jax.random.fold_in(rng, 3), *heavy), -most, most).astype(held_as)


def setup_inputs(seed: int = 0) -> dict:
    key_list = jax.random.split(jax.random.key(seed), 12)
    return {
        "inputs": draw_inputs(jax.random.fold_in(key_list[11], 71), 0),
        "w_qkv": draw_w_qkv(jax.random.fold_in(key_list[11], 71), 0),
        "w_out": gaussian(key_list[2], (D, D), (max(1, D * 8 // SEQ)) ** -0.5, 2.0, ((0, 2), (1, 4))),
        "w_up": gaussian(key_list[3], (D, FF), D ** -0.5, 0.1875, ((0, 2), (1, 4))),
        "w_down": gaussian(key_list[4], (D, FF), FF ** -0.5, 0.09375, ((0, 2), (1, 4))),
        "head_bias": gaussian(key_list[5], (2, D), 0.5, 3.0, ((1, 4),), jnp.float32),
        "up_bias": gaussian(key_list[6], (FF,), 0.5, 3.0, ((0, 4),), jnp.float32),
        "out_biases": gaussian(key_list[7], (2, D), 0.5, 3.0, (), jnp.float32),
        "norm_gains": jnp.clip(1.0 + 0.18 * jax.random.normal(key_list[8], (2, D), jnp.float32), 0.1, 1.9),
        "norm_shifts": gaussian(key_list[9], (2, D), 0.5, 3.0, (), jnp.float32),
        "cotangent": bell_draw_with(key_list[10], (SEQS, SEQ, D), 1.0, 6.0, ((0, 2), (1, 4)), (1, 2, 4, 2.0)),
    }


norm_epsilon = 1e-05
inv_root_two = 1.0 / math.sqrt(2.0)
inv_root_tau = 1.0 / math.sqrt(2.0 * math.pi)

def layer_stats(hidden):
    mean_row = lax.optimization_barrier(jnp.mean(hidden, axis=-1, keepdims=True))
    centred = hidden - mean_row
    inverse_spread = lax.rsqrt(lax.optimization_barrier(jnp.mean(centred * centred, axis=-1, keepdims=True)) + norm_epsilon)
    return (centred * inverse_spread, inverse_spread)

def layer_back(grad_norm, normed, inverse_spread):
    return inverse_spread * (grad_norm - lax.optimization_barrier(jnp.mean(grad_norm, axis=-1, keepdims=True)) - normed * lax.optimization_barrier(jnp.mean(grad_norm * normed, axis=-1, keepdims=True)))

def gelu_value(pre_act):
    return 0.5 * pre_act * (1.0 + lax.erf(pre_act * inv_root_two))

def gelu_slope(pre_act):
    return 0.5 * (1.0 + lax.erf(pre_act * inv_root_two)) + pre_act * jnp.exp(-0.5 * pre_act * pre_act) * inv_root_tau

def reference(inputs, w_qkv, w_out, w_up, w_down, head_bias, up_bias, out_biases, norm_gains, norm_shifts, cotangent):
    scale_factor = HD ** (-0.5)
    qkv_flat = w_qkv.reshape(D, 3 * D)
    block_size = math.gcd(512, SEQ)
    block_count = SEQ // block_size

    def by_heads(source):
        return source.reshape(SEQ, H, HD).transpose(1, 0, 2)

    def from_heads(source):
        return source.transpose(1, 0, 2).reshape(SEQ, D)

    def attend_head(head_args):
        query_head, key_head, value_head = head_args

        def one_block(query_block):
            scores = jnp.dot(query_block, key_head.T, preferred_element_type=jnp.float32) * scale_factor
            top_row = lax.optimization_barrier(jnp.max(scores, axis=1, keepdims=True))
            log_sum = top_row + jnp.log(lax.optimization_barrier(jnp.sum(jnp.exp(scores - top_row), axis=1, keepdims=True)))
            weights = jnp.exp(scores - log_sum).astype(jnp.bfloat16)
            return (jnp.dot(weights, value_head, preferred_element_type=jnp.float32), log_sum[:, 0])
        outputs, row_sums = lax.map(one_block, query_head.reshape(block_count, block_size, HD))
        return (outputs.reshape(SEQ, HD), row_sums.reshape(SEQ))

    def back_head(head_args):
        query_head, key_head, value_head, grad_head, sum_head, delta_head = head_args

        def step_block(state_in, block_args):
            grad_keys, grad_values = state_in
            query_block, grad_block, sum_block, delta_block = block_args
            scores = jnp.dot(query_block, key_head.T, preferred_element_type=jnp.float32) * scale_factor
            weights = jnp.exp(scores - sum_block[:, None])
            grad_values = grad_values + jnp.dot(weights.astype(jnp.bfloat16).T, grad_block, preferred_element_type=jnp.float32)
            grad_weights = jnp.dot(grad_block, value_head.T, preferred_element_type=jnp.float32)
            grad_scores = (weights * (grad_weights - delta_block[:, None]) * scale_factor).astype(jnp.bfloat16)
            grad_keys = grad_keys + jnp.dot(grad_scores.T, query_block, preferred_element_type=jnp.float32)
            return ((grad_keys, grad_values), jnp.dot(grad_scores, key_head, preferred_element_type=jnp.float32))
        zeros_head = jnp.zeros((SEQ, HD), jnp.float32)
        block_args = (query_head.reshape(block_count, block_size, HD), grad_head.reshape(block_count, block_size, HD), sum_head.reshape(block_count, block_size), delta_head.reshape(block_count, block_size))
        (grad_keys, grad_values), grad_queries = lax.scan(step_block, (zeros_head, zeros_head), block_args)
        return (grad_queries.reshape(SEQ, HD), grad_keys, grad_values)

    def one_sequence(sequence_args):
        tokens, grad_layer = sequence_args
        tokens_wide = tokens.astype(jnp.float32)
        projected = jnp.dot(tokens, qkv_flat, preferred_element_type=jnp.float32)
        queries = (projected[:, :D] + head_bias[0]).astype(jnp.bfloat16)
        keys_flat = projected[:, D:2 * D].astype(jnp.bfloat16)
        values_flat = (projected[:, 2 * D:] + head_bias[1]).astype(jnp.bfloat16)
        query_heads = by_heads(queries)
        key_heads = by_heads(keys_flat)
        value_heads = by_heads(values_flat)
        attended_heads, log_sums = lax.map(attend_head, (query_heads, key_heads, value_heads))
        attended = from_heads(attended_heads).astype(jnp.bfloat16)
        hidden_one = tokens_wide + jnp.dot(attended, w_out.T, preferred_element_type=jnp.float32) + out_biases[0]
        normed_one, inverse_one = layer_stats(hidden_one)
        mixed_one = normed_one * norm_gains[0] + norm_shifts[0]
        mixed_bf = mixed_one.astype(jnp.bfloat16)
        pre_act = jnp.dot(mixed_bf, w_up, preferred_element_type=jnp.float32) + up_bias
        gelu_bf = gelu_value(pre_act).astype(jnp.bfloat16)
        hidden_two = mixed_one + jnp.dot(gelu_bf, w_down.T, preferred_element_type=jnp.float32) + out_biases[1]
        normed_two, inverse_two = layer_stats(hidden_two)
        layer_out = (normed_two * norm_gains[1] + norm_shifts[1]).astype(jnp.bfloat16)
        grad_out = grad_layer.astype(jnp.float32)
        grad_hidden_two = layer_back(grad_out * norm_gains[1], normed_two, inverse_two)
        gain_two = lax.optimization_barrier(jnp.sum(grad_out * normed_two, axis=0))
        shift_two = lax.optimization_barrier(jnp.sum(grad_out, axis=0))
        bias_down = lax.optimization_barrier(jnp.sum(grad_hidden_two, axis=0))
        grad_two_bf = grad_hidden_two.astype(jnp.bfloat16)
        grad_down_w = jnp.dot(grad_two_bf.T, gelu_bf, preferred_element_type=jnp.float32)
        grad_pre = jnp.dot(grad_two_bf, w_down, preferred_element_type=jnp.float32) * gelu_slope(pre_act)
        grad_up_b = lax.optimization_barrier(jnp.sum(grad_pre, axis=0))
        grad_pre_bf = grad_pre.astype(jnp.bfloat16)
        grad_up_w = jnp.dot(mixed_bf.T, grad_pre_bf, preferred_element_type=jnp.float32)
        grad_mixed_one = grad_hidden_two + jnp.dot(grad_pre_bf, w_up.T, preferred_element_type=jnp.float32)
        gain_one = lax.optimization_barrier(jnp.sum(grad_mixed_one * normed_one, axis=0))
        shift_one = lax.optimization_barrier(jnp.sum(grad_mixed_one, axis=0))
        grad_hidden_one = layer_back(grad_mixed_one * norm_gains[0], normed_one, inverse_one)
        bias_out = lax.optimization_barrier(jnp.sum(grad_hidden_one, axis=0))
        grad_one_bf = grad_hidden_one.astype(jnp.bfloat16)
        grad_out_w = jnp.dot(grad_one_bf.T, attended, preferred_element_type=jnp.float32)
        grad_attended = jnp.dot(grad_one_bf, w_out, preferred_element_type=jnp.float32).astype(jnp.bfloat16)
        grad_attended_heads = by_heads(grad_attended)
        row_delta = lax.optimization_barrier(jnp.sum(grad_attended_heads.astype(jnp.float32) * by_heads(attended).astype(jnp.float32), axis=2))
        grad_query_heads, grad_key_heads, grad_value_heads = lax.map(back_head, (query_heads, key_heads, value_heads, grad_attended_heads, log_sums, row_delta))
        grad_queries = from_heads(grad_query_heads)
        grad_keys = from_heads(grad_key_heads)
        grad_values = from_heads(grad_value_heads)
        grad_heads_bias = jnp.stack([lax.optimization_barrier(jnp.sum(grad_queries, axis=0)), lax.optimization_barrier(jnp.sum(grad_values, axis=0))])
        grad_qkv_bf = jnp.concatenate([grad_queries, grad_keys, grad_values], axis=1).astype(jnp.bfloat16)
        grad_qkv_w = jnp.dot(tokens.T, grad_qkv_bf, preferred_element_type=jnp.float32).reshape(D, 3, D)
        grad_tokens = (grad_hidden_one + jnp.dot(grad_qkv_bf, qkv_flat.T, preferred_element_type=jnp.float32)).astype(jnp.bfloat16)
        return (layer_out, grad_tokens, grad_qkv_w, grad_out_w, grad_up_w, grad_down_w, grad_heads_bias, grad_up_b, jnp.stack([bias_out, bias_down]), jnp.stack([gain_one, gain_two]), jnp.stack([shift_one, shift_two]))
    results = lax.map(one_sequence, (inputs, cotangent))
    summed = [lax.optimization_barrier(jnp.sum(item, axis=0)) for item in results[2:]]
    return (results[0], results[1], summed[0], summed[1], summed[2], summed[3], summed[4], summed[5], summed[6], summed[7], summed[8])
```

```python
import math

import jax
import jax.numpy as jnp
from jax import lax
from jax.experimental import pallas as pl
from jax.experimental.pallas import tpu as pltpu
from jax.sharding import PartitionSpec as P

HD = 64
BF = jnp.bfloat16
F32 = jnp.float32


norm_epsilon = 1e-05
inv_root_two = 1.0 / math.sqrt(2.0)
inv_root_tau = 1.0 / math.sqrt(2.0 * math.pi)

NT = (((1,), (1,)), ((), ()))
NN = (((1,), (0,)), ((), ()))
TN = (((0,), (0,)), ((), ()))


def dot(a, b, dims):
    return lax.dot_general(a, b, dims, preferred_element_type=F32)


def layer_stats(hidden):
    mean_row = jnp.mean(hidden, axis=-1, keepdims=True)
    centred = hidden - mean_row
    inverse_spread = lax.rsqrt(jnp.mean(centred * centred, axis=-1, keepdims=True) + norm_epsilon)
    return (centred * inverse_spread, inverse_spread)


def layer_back(grad_norm, normed, inverse_spread):
    return inverse_spread * (
        grad_norm
        - jnp.mean(grad_norm, axis=-1, keepdims=True)
        - normed * jnp.mean(grad_norm * normed, axis=-1, keepdims=True)
    )


def gelu_value(pre_act):
    return 0.5 * pre_act * (1.0 + lax.erf(pre_act * inv_root_two))


def gelu_slope(pre_act):
    return (
        0.5 * (1.0 + lax.erf(pre_act * inv_root_two))
        + pre_act * jnp.exp(-0.5 * pre_act * pre_act) * inv_root_tau
    )


def head_mask(shape, head):
    lane = lax.broadcasted_iota(jnp.int32, shape, 1)
    return (lane >= head * HD) & (lane < (head + 1) * HD)


def as_rows(columns, rows):
    tokens = columns[0].shape[0]
    lane = lax.broadcasted_iota(jnp.int32, (tokens, 128), 1)
    tile = jnp.zeros((tokens, 128), F32)
    for i, col in enumerate(columns):
        tile = jnp.where(lane == i, col, tile)
    return tile.T[:rows]


def attend_kernel(n, heads, *refs):
    q_ref, k_refs, v_refs = refs[0], refs[1 : 1 + n], refs[1 + n : 1 + 2 * n]
    out_ref, lse_ref = refs[1 + 2 * n :]
    q = q_ref[...]
    out = jnp.zeros(q.shape, F32)
    lses = []
    for h in range(heads):
        mask = head_mask(q.shape, h)
        qh = jnp.where(mask, q, jnp.zeros_like(q))
        scores = [dot(qh, k[...], NT) for k in k_refs]
        top = scores[0]
        for s in scores[1:]:
            top = jnp.maximum(top, s)
        top = jnp.max(top, axis=1, keepdims=True)
        total = jnp.zeros(top.shape, F32)
        acc = jnp.zeros(q.shape, F32)
        psum = None
        for s, v in zip(scores, v_refs):
            p = jnp.exp(s - top)
            psum = p if psum is None else psum + p
            acc = acc + dot(p.astype(BF), v[...], NN)
        total = jnp.sum(psum, axis=1, keepdims=True)
        out = jnp.where(mask, acc / total, out)
        lses.append(top + jnp.log(total))
    out_ref[...] = out.astype(BF)
    lse_ref[...] = as_rows(lses, heads)


def attend(q, ks, vs):
    n, (tokens, cols) = len(ks), q.shape
    heads = cols // HD
    keys = n * tokens
    return pl.pallas_call(
        lambda *r: attend_kernel(n, heads, *r),
        out_shape=(
            jax.ShapeDtypeStruct((tokens, cols), BF),
            jax.ShapeDtypeStruct((heads, tokens), F32),
        ),
        cost_estimate=pl.CostEstimate(
            flops=4 * tokens * keys * cols * heads,
            bytes_accessed=2 * (2 * keys + 2 * tokens) * cols,
            transcendentals=tokens * keys * heads,
        ),
        name="attend",
    )(q, *ks, *vs)


def query_kernel(n, heads, *refs):
    q_ref, da_ref, at_ref, lse_ref = refs[:4]
    k_refs, v_refs = refs[4 : 4 + n], refs[4 + n : 4 + 2 * n]
    dq_ref, delta_ref = refs[4 + 2 * n :]
    q, da = q_ref[...], da_ref[...]
    prod = da.astype(F32) * at_ref[...].astype(F32)
    lse_cols = lse_ref[...]
    tokens = q.shape[0]
    lse_pad = jnp.concatenate([lse_cols, jnp.zeros((128 - heads, tokens), F32)], axis=0).T
    out = jnp.zeros(q.shape, F32)
    deltas = []
    for h in range(heads):
        mask = head_mask(q.shape, h)
        zero = jnp.zeros_like(q)
        qh, dah = jnp.where(mask, q, zero), jnp.where(mask, da, zero)
        delta = jnp.sum(jnp.where(mask, prod, 0.0), axis=1, keepdims=True)
        deltas.append(delta)
        lse = lse_pad[:, h : h + 1]
        acc = jnp.zeros(q.shape, F32)
        for k, v in zip(k_refs, v_refs):
            p = jnp.exp(dot(qh, k[...], NT) - lse)
            ds = (p * (dot(dah, v[...], NT) - delta)).astype(BF)
            acc = acc + dot(ds, k[...], NN)
        out = jnp.where(mask, acc, out)
    dq_ref[...] = out * (HD**-0.5)
    delta_ref[...] = as_rows(deltas, heads)


def query_grads(q, da, attended, lse, ks, vs):
    n, (tokens, cols) = len(ks), q.shape
    heads, keys = cols // HD, len(ks) * q.shape[0]
    return pl.pallas_call(
        lambda *r: query_kernel(n, heads, *r),
        out_shape=(
            jax.ShapeDtypeStruct((tokens, cols), F32),
            jax.ShapeDtypeStruct((heads, tokens), F32),
        ),
        cost_estimate=pl.CostEstimate(
            flops=6 * tokens * keys * cols * heads,
            bytes_accessed=2 * (2 * keys + 4 * tokens) * cols,
            transcendentals=tokens * keys * heads,
        ),
        name="query_grads",
    )(q, da, attended, lse, *ks, *vs)


def key_kernel(n, heads, *refs):
    k_ref, v_ref = refs[:2]
    q_refs, da_refs = refs[2 : 2 + n], refs[2 + n : 2 + 2 * n]
    lse_refs, delta_refs = refs[2 + 2 * n : 2 + 3 * n], refs[2 + 3 * n : 2 + 4 * n]
    dk_ref, dv_ref = refs[2 + 4 * n :]
    k, v = k_ref[...], v_ref[...]
    dk, dv = jnp.zeros(k.shape, F32), jnp.zeros(k.shape, F32)
    for h in range(heads):
        mask = head_mask(k.shape, h)
        zero = jnp.zeros_like(k)
        kh, vh = jnp.where(mask, k, zero), jnp.where(mask, v, zero)
        dk_acc, dv_acc = jnp.zeros(k.shape, F32), jnp.zeros(k.shape, F32)
        for q, da, lse, delta in zip(q_refs, da_refs, lse_refs, delta_refs):
            p = jnp.exp(dot(kh, q[...], NT) - lse[h : h + 1, :])
            dv_acc = dv_acc + dot(p.astype(BF), da[...], NN)
            ds = (p * (dot(vh, da[...], NT) - delta[h : h + 1, :])).astype(BF)
            dk_acc = dk_acc + dot(ds, q[...], NN)
        dk, dv = jnp.where(mask, dk_acc, dk), jnp.where(mask, dv_acc, dv)
    dk_ref[...] = dk
    dv_ref[...] = dv


def key_grads(k, v, qs, das, lses, deltas):
    n, (tokens, cols) = len(qs), k.shape
    heads, rows = cols // HD, len(qs) * k.shape[0]
    return pl.pallas_call(
        lambda *r: key_kernel(n, heads, *r),
        out_shape=(
            jax.ShapeDtypeStruct((tokens, cols), F32),
            jax.ShapeDtypeStruct((tokens, cols), F32),
        ),
        cost_estimate=pl.CostEstimate(
            flops=8 * tokens * rows * cols * heads,
            bytes_accessed=2 * (2 * rows + 4 * tokens) * cols,
            transcendentals=tokens * rows * heads,
        ),
        name="key_grads",
    )(k, v, *qs, *das, *lses, *deltas)


def build(nw, nc, nt):
    if nw != 2 or nt % 2 or nc & (nc - 1) or nt & (nt - 1):
        raise ValueError("mesh")

    def flip(axis, size, bit):
        return lambda a: lax.ppermute(a, axis, [(i, i ^ bit) for i in range(size)])

    across = flip("weight", nw, 1)
    core_swap = flip("tensor", nt, 1)

    def shifted(a, step):
        return lax.ppermute(a, "ctx", [(i, (i + step) % nc) for i in range(nc)])

    def gather(a):
        return [a] + [shifted(a, s) for s in range(1, nc)]

    def settle(partial):
        half = partial.shape[0] // 2
        total = partial[:half] + core_swap(partial[half:].astype(BF)).astype(F32)
        bit = 2
        while bit < nt:
            sent = total.astype(BF)
            total = lax.reduce_precision(total, 8, 7) + flip("tensor", nt, bit)(sent).astype(F32)
            bit *= 2
        return total

    def both_halves(own):
        return jnp.concatenate([own, core_swap(own)], axis=0)

    def owned(grad):
        rank = lax.axis_index("ctx")
        rows = grad.shape[0] // nc
        grad = grad.astype(BF)
        total = lax.dynamic_slice_in_dim(grad, rank * rows, rows, 0).astype(F32)
        for s in range(1, nc):
            part = lax.dynamic_slice_in_dim(grad, ((rank + s) % nc) * rows, rows, 0)
            total = total + shifted(part, s).astype(F32)
        return total

    def local(
        inputs, w_qkv, w_out, w_up, w_down, head_bias, up_bias, out_biases,
        norm_gains, norm_shifts, cotangent,
    ):
        tokens, width = inputs.shape[1], inputs.shape[2]
        half_t, half_d = tokens // 2, width // 2
        cols = w_qkv.shape[2]
        far_weight = lax.axis_index("weight") == 1
        far_core = lax.axis_index("tensor") % 2 == 1

        def turn_d(a):
            return jnp.where(far_weight, jnp.concatenate([a[:, half_d:], a[:, :half_d]], 1), a)

        def turn_t(a):
            return jnp.where(far_core, jnp.concatenate([a[half_t:], a[:half_t]], 0), a)

        x = turn_t(turn_d(inputs[0]))
        cot = turn_t(turn_d(cotangent[0]))[:half_t].astype(F32)
        out_b, gains, shifts = turn_d(out_biases), turn_d(norm_gains), turn_d(norm_shifts)

        wk, wv, wq = w_qkv[:, 1], w_qkv[:, 2], w_qkv[:, 0]
        wk_far, wv_far, wq_far = across(wk), across(wv), across(wq)
        out_far, up_far, down_far = across(w_out), across(w_up), across(w_down)

        x_lo, x_hi = x[:, :half_d], x[:, half_d:]

        def project(near, far):
            return dot(x_lo, near, NN) + dot(x_hi, far, NN)

        k = project(wk, wk_far).astype(BF)
        ks = gather(k)
        v = (project(wv, wv_far) + head_bias[1]).astype(BF)
        vs = gather(v)
        q = (project(wq, wq_far) + head_bias[0]).astype(BF) * BF(HD**-0.5)
        qs = gather(q)
        x_mate = both_halves(across(x[:half_t, half_d:]))

        attended, lse = attend(q, ks, vs)
        lses = gather(lse)
        attended_mate = across(attended)

        def spread(a, near, far):
            return jnp.concatenate([dot(a, near, NT), dot(a, far, NT)], axis=1)

        hidden_one = x[:half_t].astype(F32) + settle(spread(attended, w_out, out_far)) + out_b[0]
        normed_one, inverse_one = layer_stats(hidden_one)
        mixed_one = normed_one * gains[0] + shifts[0]
        mixed_own = mixed_one.astype(BF)
        mixed = both_halves(mixed_own)
        mixed_mate = both_halves(across(mixed_own[:, half_d:]))
        pre_act = (
            dot(mixed[:, :half_d], w_up, NN) + dot(mixed[:, half_d:], up_far, NN) + up_bias
        )
        act = gelu_value(pre_act).astype(BF)
        act_mate = across(act)
        hidden_two = mixed_one + settle(spread(act, w_down, down_far)) + out_b[1]
        normed_two, inverse_two = layer_stats(hidden_two)
        layer_out = (normed_two * gains[1] + shifts[1]).astype(BF)
        layer_out = turn_d(turn_t(both_halves(layer_out)))

        grad_two = layer_back(cot * gains[1], normed_two, inverse_two)
        gain_two = jnp.sum(cot * normed_two, axis=0)
        shift_two = jnp.sum(cot, axis=0)
        bias_down = jnp.sum(grad_two, axis=0)
        two_own = grad_two.astype(BF)
        two = both_halves(two_own)
        two_mate = both_halves(across(two_own[:, half_d:]))
        grad_act = dot(two[:, :half_d], w_down, NN) + dot(two[:, half_d:], down_far, NN)
        grad_pre = grad_act * gelu_slope(pre_act)
        grad_up_b = jnp.sum(grad_pre, axis=0)
        pre_bf = grad_pre.astype(BF)
        pre_mate = across(pre_bf)
        mixed_sum = settle(spread(pre_bf, w_up, up_far))
        grad_w_down = owned(dot(two[:, :half_d], act, TN) + dot(two_mate, act_mate, TN))

        grad_mixed = grad_two + mixed_sum
        grad_one = layer_back(grad_mixed * gains[0], normed_one, inverse_one)
        gain_one = jnp.sum(grad_mixed * normed_one, axis=0)
        shift_one = jnp.sum(grad_mixed, axis=0)
        bias_out = jnp.sum(grad_one, axis=0)
        one_own = grad_one.astype(BF)
        one = both_halves(one_own)
        one_mate = both_halves(across(one_own[:, half_d:]))
        da = (dot(one[:, :half_d], w_out, NN) + dot(one[:, half_d:], out_far, NN)).astype(BF)
        das = gather(da)
        dq, delta = query_grads(q, da, attended, lse, ks, vs)
        deltas = gather(delta)
        dq_bf = dq.astype(BF)
        dq_mate = across(dq_bf)

        up_grad = dot(mixed[:, :half_d], pre_bf, TN) + dot(mixed_mate, pre_mate, TN)
        up_grad, das[0] = lax.optimization_barrier((up_grad.astype(BF), das[0]))
        grad_w_up = owned(up_grad)
        grad_w_out = owned(dot(one[:, :half_d], attended, TN) + dot(one_mate, attended_mate, TN))
        grad_wq = owned(dot(x_lo, dq_bf, TN) + dot(x_mate, dq_mate, TN))

        dk, dv = key_grads(k, v, qs, das, lses, deltas)
        dk_bf, dv_bf = dk.astype(BF), dv.astype(BF)
        dk_mate, dv_mate = across(dk_bf), across(dv_bf)
        near = dot(dq_bf, wq, NT) + dot(dk_bf, wk, NT) + dot(dv_bf, wv, NT)
        far = dot(dq_bf, wq_far, NT) + dot(dk_bf, wk_far, NT) + dot(dv_bf, wv_far, NT)
        grad_in = (grad_one + settle(jnp.concatenate([near, far], axis=1))).astype(BF)
        grad_input = turn_d(turn_t(both_halves(grad_in)))
        grad_wk = owned(dot(x_lo, dk_bf, TN) + dot(x_mate, dk_mate, TN))
        grad_wv = owned(dot(x_lo, dv_bf, TN) + dot(x_mate, dv_mate, TN))

        def everywhere(a):
            a = a + across(a)
            bit = 1
            while bit < nc:
                a = a + flip("ctx", nc, bit)(a)
                bit *= 2
            return a

        rows = jnp.stack([bias_out, bias_down, gain_one, gain_two, shift_one, shift_two])
        rows = turn_d(rows + core_swap(rows))
        rows = everywhere(rows)
        grad_up_b = everywhere(grad_up_b.reshape(-1, 128)).reshape(-1)
        grad_head_b = everywhere(jnp.stack([jnp.sum(dq, axis=0), jnp.sum(dv, axis=0)]))
        return (
            layer_out[None],
            grad_input[None],
            jnp.stack([grad_wq, grad_wk, grad_wv], axis=1),
            grad_w_out,
            grad_w_up,
            grad_w_down,
            grad_head_b,
            grad_up_b,
            rows[0:2],
            rows[2:4],
            rows[4:6],
        )

    return local


def solution(mesh):
    return jax.shard_map(
        build(mesh.shape["weight"], mesh.shape["ctx"], mesh.shape["tensor"]),
        mesh=mesh,
        in_specs=(
            P("weight", "ctx", None),
            P("weight", None, "tensor"),
            P("weight", "tensor"),
            P("weight", "tensor"),
            P("weight", "tensor"),
            P(None, "tensor"),
            P("tensor"),
            P(),
            P(),
            P(),
            P("weight", "ctx", None),
        ),
        out_specs=(
            P("weight", "ctx", None),
            P("weight", "ctx", None),
            P(("weight", "ctx"), None, "tensor"),
            P(("weight", "ctx"), "tensor"),
            P(("weight", "ctx"), "tensor"),
            P(("weight", "ctx"), "tensor"),
            P(None, "tensor"),
            P("tensor"),
            P(),
            P(),
            P(),
        ),
        check_vma=False,
    )
```

```python
import math

import jax
import jax.numpy as jnp
from jax import lax
from jax.experimental import pallas as pl
from jax.experimental.pallas import tpu as pltpu
from jax.sharding import PartitionSpec as P


HD = 64
ROOM = pltpu.CompilerParams(vmem_limit_bytes=20 << 20)
BF = jnp.bfloat16
F32 = jnp.float32


norm_epsilon = 1e-05
inv_root_two = 1.0 / math.sqrt(2.0)
inv_root_tau = 1.0 / math.sqrt(2.0 * math.pi)

NT = (((1,), (1,)), ((), ()))
NN = (((1,), (0,)), ((), ()))
TN = (((0,), (0,)), ((), ()))


def dot(a, b, dims):
    return lax.dot_general(a, b, dims, preferred_element_type=F32)


def layer_stats(hidden):
    mean_row = jnp.mean(hidden, axis=-1, keepdims=True)
    centred = hidden - mean_row
    inverse_spread = lax.rsqrt(jnp.mean(centred * centred, axis=-1, keepdims=True) + norm_epsilon)
    return (centred * inverse_spread, inverse_spread)


def layer_back(grad_norm, normed, inverse_spread):
    return inverse_spread * (
        grad_norm
        - jnp.mean(grad_norm, axis=-1, keepdims=True)
        - normed * jnp.mean(grad_norm * normed, axis=-1, keepdims=True)
    )


def gelu_value(pre_act):
    return 0.5 * pre_act * (1.0 + lax.erf(pre_act * inv_root_two))


def gelu_slope(pre_act):
    return (
        0.5 * (1.0 + lax.erf(pre_act * inv_root_two))
        + pre_act * jnp.exp(-0.5 * pre_act * pre_act) * inv_root_tau
    )


def head_mask(shape, head):
    lane = lax.broadcasted_iota(jnp.int32, shape, 1)
    return (lane >= head * HD) & (lane < (head + 1) * HD)


def as_rows(columns, rows):
    tokens = columns[0].shape[0]
    lane = lax.broadcasted_iota(jnp.int32, (tokens, 128), 1)
    tile = jnp.zeros((tokens, 128), F32)
    for i, col in enumerate(columns):
        tile = jnp.where(lane == i, col, tile)
    return tile.T[:rows]


def halves(refs):
    cols = refs[0].shape[1] // 2
    return [r.at[:, pl.ds(0, cols)] for r in refs], [r.at[:, pl.ds(cols, cols)] for r in refs]


def attend_kernel(n, heads, *refs):
    q_ref, near_ref, far_ref, kv_refs = refs[0], refs[1], refs[2], refs[3 : 3 + n]
    out_ref, lse_ref, keep_ref, sent_ref = refs[3 + n :]
    q = q_ref[...]
    k_refs, v_refs = halves(kv_refs)
    out = jnp.zeros(q.shape, F32)
    lses = []
    for h in range(heads):
        mask = head_mask(q.shape, h)
        qh = jnp.where(mask, q, jnp.zeros_like(q))
        scores = [dot(qh, k[...], NT) for k in k_refs]
        top = scores[0]
        for s in scores[1:]:
            top = jnp.maximum(top, s)
        top = jnp.max(top, axis=1, keepdims=True)
        total = jnp.zeros(top.shape, F32)
        acc = jnp.zeros(q.shape, F32)
        psum = None
        for s, v in zip(scores, v_refs):
            p = jnp.exp(s - top)
            psum = p if psum is None else psum + p
            acc = acc + dot(p.astype(BF), v[...], NN)
        total = jnp.sum(psum, axis=1, keepdims=True)
        out = jnp.where(mask, acc / total, out)
        lses.append(top + jnp.log(total))
    out_ref[...] = out.astype(BF)
    lse_ref[...] = as_rows(lses, heads)
    weight = pl.ds(near_ref.shape[1] - q.shape[1], q.shape[1])
    out_kernel(out_ref, near_ref.at[:, weight], far_ref.at[:, weight], keep_ref, sent_ref)


def attend(q, near, far, kvs):
    n, (tokens, cols) = len(kvs), q.shape
    width = 2 * near.shape[0]
    heads = cols // HD
    keys = n * tokens
    return pl.pallas_call(
        lambda *r: attend_kernel(n, heads, *r),
        out_shape=(
            jax.ShapeDtypeStruct((tokens, cols), BF),
            jax.ShapeDtypeStruct((heads, tokens), F32),
            jax.ShapeDtypeStruct((tokens // 2, width), F32),
            jax.ShapeDtypeStruct((tokens // 2, width), BF),
        ),
        cost_estimate=pl.CostEstimate(
            flops=4 * tokens * keys * cols * heads,
            bytes_accessed=2 * (2 * keys + 2 * tokens) * cols,
            transcendentals=tokens * keys * heads,
        ),
        name="attend",
        compiler_params=ROOM,
    )(q, near, far, *kvs)


def split_rows(rows):
    high = rows.astype(BF)
    rest = rows - high.astype(F32)
    middle = rest.astype(BF)
    low = (rest - middle.astype(F32)).astype(BF)
    return [high, middle, low]


def message_rows(tokens, heads):
    return tokens + -(-6 * heads // 16) * 16


def pack_kernel(heads, own_ref, got_ref, near_ref, far_ref, at_ref, lse_ref, msg_ref):
    half = near_ref.shape[0]
    one = jnp.concatenate([own_ref[...], got_ref[...]], axis=0)
    cols = at_ref.shape[1]
    out = pl.ds(near_ref.shape[1] - cols, cols)
    da = dot(one[:, :half], near_ref[:, out], NN) + dot(one[:, half:], far_ref[:, out], NN)
    da = da.astype(BF)
    tokens = da.shape[0]
    prod = da.astype(F32) * at_ref[...].astype(F32)
    deltas = []
    for h in range(heads):
        mask = head_mask(da.shape, h)
        deltas.append(jnp.sum(jnp.where(mask, prod, 0.0), axis=1, keepdims=True))
    rows = split_rows(lse_ref[...]) + split_rows(as_rows(deltas, heads))
    spare = msg_ref.shape[0] - tokens - 6 * heads
    if spare:
        rows.append(jnp.zeros((spare, tokens), BF))
    msg_ref[:tokens, :] = da
    msg_ref[tokens:, :] = jnp.concatenate([r.astype(F32) for r in rows], axis=0).astype(BF)


def pack_message(own, got, near, far, attended, lse):
    tokens, cols = attended.shape
    heads = cols // HD
    if tokens != cols:
        raise ValueError("message shape")
    return pl.pallas_call(
        lambda *r: pack_kernel(heads, *r),
        out_shape=jax.ShapeDtypeStruct((message_rows(tokens, heads), cols), BF),
        cost_estimate=pl.CostEstimate(
            flops=2 * tokens * own.shape[1] * cols,
            bytes_accessed=2 * (2 * own.size + near.size + far.size + 2 * attended.size),
            transcendentals=0,
        ),
        name="pack_message",
        compiler_params=ROOM,
    )(own, got, near, far, attended, lse)


def query_kernel(n, heads, *refs):
    q_ref, da_ref, at_ref, lse_ref = refs[:4]
    k_refs, v_refs = halves(refs[4 : 4 + n])
    dq_ref, sum_ref = refs[4 + n :]
    q = q_ref[...]
    tokens = q.shape[0]
    da = da_ref[:tokens, :]
    prod = da.astype(F32) * at_ref[...].astype(F32)
    lse_pad = jnp.concatenate([lse_ref[...], jnp.zeros((128 - heads, tokens), F32)], axis=0).T
    out = jnp.zeros(q.shape, F32)
    for h in range(heads):
        mask = head_mask(q.shape, h)
        zero = jnp.zeros_like(q)
        qh, dah = jnp.where(mask, q, zero), jnp.where(mask, da, zero)
        delta = jnp.sum(jnp.where(mask, prod, 0.0), axis=1, keepdims=True)
        lse = lse_pad[:, h : h + 1]
        acc = jnp.zeros(q.shape, F32)
        for k, v in zip(k_refs, v_refs):
            p = jnp.exp(dot(qh, k[...], NT) - lse)
            ds = (p * (dot(dah, v[...], NT) - delta)).astype(BF)
            acc = acc + dot(ds, k[...], NN)
        out = jnp.where(mask, acc, out)
    out = out * (HD**-0.5)
    dq_ref[...] = out.astype(BF)
    sum_ref[...] = jnp.sum(out, axis=0, keepdims=True)


def query_grads(q, msg, attended, lse, kvs):
    n, (tokens, cols) = len(kvs), q.shape
    heads, keys = cols // HD, len(kvs) * q.shape[0]
    return pl.pallas_call(
        lambda *r: query_kernel(n, heads, *r),
        out_shape=(
            jax.ShapeDtypeStruct((tokens, cols), BF),
            jax.ShapeDtypeStruct((1, cols), F32),
        ),
        cost_estimate=pl.CostEstimate(
            flops=6 * tokens * keys * cols * heads,
            bytes_accessed=2 * (2 * keys + 4 * tokens) * cols,
            transcendentals=tokens * keys * heads,
        ),
        name="query_grads",
        compiler_params=ROOM,
    )(q, msg, attended, lse, *kvs)


def key_kernel(m, n, heads, *refs):
    kv_ref = refs[0]
    tokens, cols = kv_ref.shape[0], kv_ref.shape[1] // 2
    qs = [
        r.at[pl.ds(i * tokens, tokens)]
        for r in refs[1 : 1 + m]
        for i in range(r.shape[0] // tokens)
    ]
    msgs = refs[1 + m : 1 + m + n]
    out_ref, sum_ref = refs[1 + m + n :]
    k, v = kv_ref[:, :cols], kv_ref[:, cols:]
    stats = []
    for msg in msgs:
        rows = msg[tokens:, :].astype(F32)
        part = [rows[i * heads : (i + 1) * heads] for i in range(6)]
        stats.append((part[0] + part[1] + part[2], part[3] + part[4] + part[5]))
    dk, dv = jnp.zeros(k.shape, F32), jnp.zeros(k.shape, F32)
    for h in range(heads):
        mask = head_mask(k.shape, h)
        zero = jnp.zeros_like(k)
        kh, vh = jnp.where(mask, k, zero), jnp.where(mask, v, zero)
        dk_acc, dv_acc = jnp.zeros(k.shape, F32), jnp.zeros(k.shape, F32)
        for q, msg, (lse, delta) in zip(qs, msgs, stats):
            da = msg[:tokens, :]
            p = jnp.exp(dot(kh, q[...], NT) - lse[h : h + 1, :])
            dv_acc = dv_acc + dot(p.astype(BF), da, NN)
            ds = (p * (dot(vh, da, NT) - delta[h : h + 1, :])).astype(BF)
            dk_acc = dk_acc + dot(ds, q[...], NN)
        dk, dv = jnp.where(mask, dk_acc, dk), jnp.where(mask, dv_acc, dv)
    out_ref[:, :cols] = dk.astype(BF)
    out_ref[:, cols:] = dv.astype(BF)
    sum_ref[...] = jnp.sum(dv, axis=0, keepdims=True)


def key_grads(kv, qs, msgs):
    m, n, tokens, cols = len(qs), len(msgs), kv.shape[0], kv.shape[1] // 2
    heads, rows = cols // HD, n * tokens
    return pl.pallas_call(
        lambda *r: key_kernel(m, n, heads, *r),
        out_shape=(
            jax.ShapeDtypeStruct((tokens, 2 * cols), BF),
            jax.ShapeDtypeStruct((1, cols), F32),
        ),
        cost_estimate=pl.CostEstimate(
            flops=8 * tokens * rows * cols * heads,
            bytes_accessed=2 * (2 * rows + 4 * tokens) * cols,
            transcendentals=tokens * rows * heads,
        ),
        name="key_grads",
        compiler_params=ROOM,
    )(kv, *qs, *msgs)


def shape(rows, cols, dtype):
    return jax.ShapeDtypeStruct((rows, cols), dtype)


def call(kernel, outs, *args, flops=0, scalars=0):
    outs_list = outs if isinstance(outs, (tuple, list)) else (outs,)
    total = sum(math.prod(a.shape) * a.dtype.itemsize for a in list(args) + list(outs_list))
    return pl.pallas_call(
        kernel,
        out_shape=outs,
        in_specs=[
            pl.BlockSpec(memory_space=pltpu.SMEM if i < scalars else pltpu.VMEM)
            for i in range(len(args))
        ],
        cost_estimate=pl.CostEstimate(flops=flops, bytes_accessed=total, transcendentals=0),
        compiler_params=ROOM,
    )(*args)


def column_blocks(cols):
    size = 256 if cols % 256 == 0 else cols
    return [pl.ds(i, size) for i in range(0, cols, size)]


def put_partial(block, value, keep_ref, sent_ref):
    half = keep_ref.shape[0]
    keep_ref[:, block] = value[:half]
    sent_ref[:, block] = value[half:].astype(BF)


def out_kernel(at_ref, near_ref, far_ref, keep_ref, sent_ref):
    at = at_ref[...]
    half = near_ref.shape[0]
    for start, ref in ((0, near_ref), (half, far_ref)):
        for rows in column_blocks(half):
            value = dot(at, ref[rows, :], NT)
            put_partial(pl.ds(start + rows.start, rows.size), value, keep_ref, sent_ref)


def norm_one_kernel(sent_ref, got_ref, x_ref, bias_ref, gain_ref, shift_ref, *outs):
    mixed_ref, normed_ref, inverse_ref, own_ref = outs
    summed = sent_ref[...].astype(F32) + got_ref[...].astype(F32)
    hidden = x_ref[...].astype(F32) + summed + bias_ref[0:1, :]
    normed, inverse = layer_stats(hidden)
    mixed = normed * gain_ref[0:1, :] + shift_ref[0:1, :]
    mixed_ref[...] = mixed
    normed_ref[...] = normed
    inverse_ref[...] = jnp.broadcast_to(inverse, inverse_ref.shape)
    own_ref[...] = mixed.astype(BF)


def up_kernel(own_ref, got_ref, near_ref, far_ref, bias_ref, pre_ref, act_ref):
    half = near_ref.shape[0]
    mixed = jnp.concatenate([own_ref[...], got_ref[...]], axis=0)
    low, high = mixed[:, :half], mixed[:, half:]
    for block in column_blocks(near_ref.shape[1]):
        pre = dot(low, near_ref[:, block], NN) + dot(high, far_ref[:, block], NN)
        pre = pre + bias_ref[:, block]
        pre_ref[:, block] = pre
        act_ref[:, block] = gelu_value(pre).astype(BF)


def offsets(n):
    held = [0]
    for bit in levels(n):
        held = held + [i ^ bit for i in held]
    return held


def down_kernel(rank_ref, act_ref, near_ref, *refs):
    pieces, (far_ref, keep_ref, sent_ref) = refs[:-3], refs[-3:]
    rows = pieces[0].shape[0]
    for offset, piece in zip(offsets(len(pieces)), pieces):
        at = pl.multiple_of(jnp.bitwise_xor(rank_ref[0], offset) * rows, rows)
        far_ref[pl.ds(at, rows), :] = piece[...]
    out_kernel(act_ref, near_ref, far_ref, keep_ref, sent_ref)


def norm_two_kernel(
    sent_ref, got_ref, mixed_ref, cot_ref, bias_ref, gain_ref, shift_ref, pair_ref, grad_ref, sum_ref
):
    summed = sent_ref[...].astype(F32) + got_ref[...].astype(F32)
    normed, inverse = layer_stats(mixed_ref[...] + summed + bias_ref[1:2, :])
    gain = gain_ref[1:2, :]
    cot = cot_ref[...].astype(F32)
    grad = layer_back(cot * gain, normed, inverse)
    half = grad.shape[0]
    pair_ref[:half, :] = grad.astype(BF)
    pair_ref[half:, :] = (normed * gain + shift_ref[1:2, :]).astype(BF)
    grad_ref[...] = grad
    sum_ref[0:1, :] = jnp.sum(grad, axis=0, keepdims=True)
    sum_ref[1:2, :] = jnp.sum(cot * normed, axis=0, keepdims=True)
    sum_ref[2:3, :] = jnp.sum(cot, axis=0, keepdims=True)


def back_kernel(own_ref, got_ref, dn_ref, df_ref, pre_ref, un_ref, uf_ref, *outs):
    grad_ref, sum_ref, keep_ref, sent_ref = outs
    half = dn_ref.shape[0]
    tokens = own_ref.shape[0] // 2
    two = jnp.concatenate([own_ref[:tokens, :], got_ref[:tokens, :]], axis=0)
    low, high = two[:, :half], two[:, half:]
    for block in column_blocks(dn_ref.shape[1]):
        grad = dot(low, dn_ref[:, block], NN) + dot(high, df_ref[:, block], NN)
        grad = grad * gelu_slope(pre_ref[:, block])
        sum_ref[:, block] = jnp.sum(grad, axis=0, keepdims=True)
        grad_ref[:, block] = grad.astype(BF)
    out_kernel(grad_ref, un_ref, uf_ref, keep_ref, sent_ref)


def norm_back_kernel(sent_ref, got_ref, two_ref, normed_ref, inverse_ref, gain_ref, *outs):
    own_ref, grad_ref, sum_ref = outs
    normed = normed_ref[...]
    mixed = two_ref[...] + (sent_ref[...].astype(F32) + got_ref[...].astype(F32))
    grad = layer_back(mixed * gain_ref[0:1, :], normed, inverse_ref[:, 0:1])
    own_ref[...] = grad.astype(BF)
    grad_ref[...] = grad
    sum_ref[0:1, :] = jnp.sum(grad, axis=0, keepdims=True)
    sum_ref[1:2, :] = jnp.sum(mixed * normed, axis=0, keepdims=True)
    sum_ref[2:3, :] = jnp.sum(mixed, axis=0, keepdims=True)


def input_kernel(dq_ref, dkv_ref, qo_ref, qo_far_ref, kv_ref, kv_far_ref, keep_ref, sent_ref):
    dq, dkv = dq_ref[...], dkv_ref[...]
    cols, half = dq.shape[1], qo_ref.shape[0]
    for start, q_ref, k_ref in ((0, qo_ref, kv_ref), (half, qo_far_ref, kv_far_ref)):
        for rows in column_blocks(half):
            value = dot(dq, q_ref[rows, pl.ds(0, cols)], NT) + dot(dkv, k_ref[rows, :], NT)
            put_partial(pl.ds(start + rows.start, rows.size), value, keep_ref, sent_ref)


def weight_kernel(n, terms, mine_ref, *refs):
    ins, (away_ref, stay_ref) = refs[:-2], refs[-2:]
    rows = away_ref.shape[1]
    mine = mine_ref[0]
    for i in range(n // 2):
        for out, side in ((away_ref, 1 - mine), (stay_ref, mine)):
            at = pl.multiple_of((2 * i + side) * rows, rows)
            col, k = 0, 0
            for count in terms:
                value = None
                for _ in range(count):
                    a, b = ins[k], ins[k + 1]
                    k += 2
                    term = dot(a[:, pl.ds(at, rows)], b[...], TN)
                    value = term if value is None else value + term
                out[i, :, pl.ds(col, value.shape[1])] = value.astype(BF)
                col += value.shape[1]


def levels(n):
    return [1 << i for i in reversed(range(n.bit_length() - 1))]


def build(nw, nc, nt):
    if nw != 2 or nt % 2 or nc & (nc - 1) or nt & (nt - 1):
        raise ValueError("mesh")
    sizes = {"weight": nw, "ctx": nc, "tensor": nt}

    def send(a, axis, bit=1):
        return lax.ppermute(a, axis, [(i, i ^ bit) for i in range(sizes[axis])])

    def settle(keep, sent):
        total = keep + send(sent, "tensor").astype(F32)
        bit = 2
        while bit < nt:
            sent = total.astype(BF)
            got = send(sent, "tensor", bit)
            total = sent.astype(F32) + got.astype(F32)
            bit *= 2
        return sent, got

    def gather(a):
        held, bit = [a], nc // 2
        while bit:
            held = held + [send(h, "ctx", bit) for h in held]
            bit //= 2
        return held

    def gather_few(a):
        held, bit = [a], nc // 2
        while bit:
            whole = held[0] if len(held) == 1 else jnp.concatenate(held, axis=0)
            held = held + [send(whole, "ctx", bit)]
            bit //= 2
        return held

    def owned(products, after):
        rank = lax.axis_index("ctx")
        rows = products[0][0][0].shape[1] // nc
        cols = sum(p[0][1].shape[1] for p in products)
        mine = jnp.bitwise_and(rank, 1)
        if rows % 128 == 0:
            flat = [m for p in products for term in p for m in term]
            terms = [len(p) for p in products]
            part = jax.ShapeDtypeStruct((nc // 2, rows, cols), BF)
            away, stay = call(
                lambda *r: weight_kernel(nc, terms, *r),
                (part, part),
                mine.reshape(1),
                *flat,
                flops=sum(2 * m.shape[0] * m.shape[1] * rows * nc for m in flat[1::2]),
                scalars=1,
            )
        else:
            grad = [sum(dot(a_, b_, TN) for a_, b_ in p).astype(BF) for p in products]
            view = jnp.concatenate(grad, axis=1).reshape(nc // 2, 2, rows, cols)
            away = lax.dynamic_index_in_dim(view, 1 - mine, 1, keepdims=False)
            stay = lax.dynamic_index_in_dim(view, mine, 1, keepdims=False)
        bit = 1
        while True:
            got = send(away, "ctx", bit)
            got, stay, _ = lax.optimization_barrier((got, stay, after[0]))
            after = after[1:]
            total = stay.astype(F32) + got.astype(F32)
            bit *= 2
            if bit == nc:
                return total.reshape(rows, cols)
            mine = jnp.bitwise_and(rank // bit, 1)
            view = total.reshape(total.shape[0] // 2, 2, rows, cols)
            away = lax.dynamic_index_in_dim(view, 1 - mine, 1, keepdims=False).astype(BF)
            stay = lax.dynamic_index_in_dim(view, mine, 1, keepdims=False)

    def local(
        inputs, w_qkv, w_out, w_up, w_down, head_bias, up_bias, out_biases,
        norm_gains, norm_shifts, cotangent,
    ):
        tokens, width = inputs.shape[1], inputs.shape[2]
        half_t, half_d = tokens // 2, width // 2
        cols, hidden = w_qkv.shape[2], w_up.shape[1]
        rank = lax.axis_index("ctx")
        far_weight = lax.axis_index("weight") == 1
        far_core = jnp.bitwise_and(lax.axis_index("tensor"), 1) == 1

        def turn_d(a):
            return jnp.where(far_weight, jnp.concatenate([a[:, half_d:], a[:, :half_d]], 1), a)

        def turn_t(a):
            return jnp.where(far_core, jnp.concatenate([a[half_t:], a[:half_t]], 0), a)

        wq = w_qkv[:, 0]
        wkv = w_qkv[:, 1:3].reshape(half_d, 2 * cols)
        wqo = jnp.concatenate([wq, w_out], axis=1)
        wkv_far = send(wkv, "weight")
        wqo_far = send(wqo, "weight")
        piece = lax.dynamic_slice_in_dim(w_down, rank * (half_d // nc), half_d // nc, 0)
        piece = send(piece, "weight")
        up_far = send(w_up, "weight")
        pieces = gather(piece)

        x = turn_t(turn_d(inputs[0]))
        x_own = x[:half_t]
        cot = turn_t(turn_d(cotangent[0]))[:half_t]
        out_b, gains, shifts = turn_d(out_biases), turn_d(norm_gains), turn_d(norm_shifts)
        x_lo, x_hi = x[:, :half_d], x[:, half_d:]

        kv_bias = jnp.concatenate([jnp.zeros((cols,), F32), head_bias[1]])
        kv = (dot(x_lo, wkv, NN) + dot(x_hi, wkv_far, NN) + kv_bias).astype(BF)
        kvs = gather(kv)
        q = dot(x_lo, wq, NN) + dot(x_hi, wqo_far[:, :cols], NN) + head_bias[0]
        q = q.astype(BF) * BF(HD**-0.5)
        qs = gather_few(q)

        part = (shape(half_t, width, F32), shape(half_t, width, BF))
        attended, lse, keep, sent = attend(q, wqo, wqo_far, kvs)
        sent, got = settle(keep, sent)
        mixed_one, normed_one, inverse_one, mixed_own = call(
            norm_one_kernel,
            (part[0], part[0], shape(half_t, 128, F32), part[1]),
            sent, got, x_own, out_b, gains, shifts,
        )
        mixed_got = send(mixed_own, "tensor")
        big = 2 * tokens * width * hidden
        pre_act, act = call(
            up_kernel,
            (shape(tokens, hidden, F32), shape(tokens, hidden, BF)),
            mixed_own, mixed_got, w_up, up_far, up_bias.reshape(1, hidden),
            flops=big,
        )
        down_far, keep, sent = call(
            down_kernel,
            (shape(half_d, hidden, BF),) + part,
            rank.reshape(1), act, w_down, *pieces,
            flops=big, scalars=1,
        )
        sent, got = settle(keep, sent)
        act_mate = send(act, "weight")
        mixed_hi = jnp.concatenate([mixed_own[:, half_d:], mixed_got[:, half_d:]], axis=0)
        bundle = send(jnp.concatenate([mixed_hi, x_hi, attended], axis=1), "weight")
        mixed_mate, x_mate = bundle[:, :half_d], bundle[:, half_d:width]
        attended_mate = bundle[:, width:]

        pair, grad_two, sums_two = call(
            norm_two_kernel,
            (shape(tokens, width, BF), part[0], shape(3, width, F32)),
            sent, got, mixed_one, cot, out_b, gains, shifts,
        )
        pair_got = send(pair, "tensor")
        two_hi = jnp.concatenate([pair[:half_t, half_d:], pair_got[:half_t, half_d:]], axis=0)
        two_mate = send(two_hi, "weight")
        grad_pre, grad_up_b, keep, sent = call(
            back_kernel,
            (shape(tokens, hidden, BF), shape(1, hidden, F32)) + part,
            pair, pair_got, w_down, down_far, pre_act, w_up, up_far,
            flops=2 * big,
        )
        sent, got = settle(keep, sent)
        pre_mate = send(grad_pre, "weight")
        one_own, grad_one, sums_one = call(
            norm_back_kernel,
            (part[1], part[0], shape(3, width, F32)),
            sent, got, grad_two, normed_one, inverse_one, gains,
        )
        one_got = send(one_own, "tensor")
        msg = pack_message(one_own, one_got, wqo, wqo_far, attended, lse)
        msgs = gather(msg)
        two_lo = jnp.concatenate([pair[:half_t, :half_d], pair_got[:half_t, :half_d]], axis=0)
        one = jnp.concatenate([one_own, one_got], axis=0)
        one_mate = send(one[:, half_d:], "weight")
        dq, sums_q = query_grads(q, msg, attended, lse, kvs)
        dq_mate = send(dq, "weight")
        mixed_lo = jnp.concatenate([mixed_own[:, :half_d], mixed_got[:, :half_d]], axis=0)
        dkv, sums_v = key_grads(kv, qs, msgs)

        dkv_mate = send(dkv, "weight")
        keep, sent = call(
            input_kernel, part, dq, dkv, wqo, wqo_far, wkv, wkv_far,
            flops=6 * tokens * width * cols,
        )
        late = [sent] * 8
        grad_w_down = owned([[(two_lo, act), (two_mate, act_mate)]], [msg] + late)
        grad_w_up = owned([[(mixed_lo, grad_pre), (mixed_mate, pre_mate)]], [dq] + late)
        oq_grad = owned(
            [
                [(one[:, :half_d], attended), (one_mate, attended_mate)],
                [(x_lo, dq), (x_mate, dq_mate)],
            ],
            late,
        )
        grad_w_out, grad_wq = oq_grad[:, :cols], oq_grad[:, cols:]
        sent, got = settle(keep, sent)
        grad_wkv = owned([[(x_lo, dkv), (x_mate, dkv_mate)]], late)
        grad_own = (grad_one + (sent.astype(F32) + got.astype(F32))).astype(BF)
        grad_got = send(grad_own, "tensor")
        grad_input = turn_d(turn_t(jnp.concatenate([grad_own, grad_got], axis=0)))
        pair, pair_got, _ = lax.optimization_barrier((pair, pair_got, late[0]))
        layer_out = turn_d(turn_t(jnp.concatenate([pair[half_t:], pair_got[half_t:]], axis=0)))

        rows = jnp.concatenate([sums_one, sums_two], axis=0)
        rows = turn_d(rows + send(rows, "tensor"))
        vector = [rows.reshape(-1), grad_up_b[0], sums_q[0], sums_v[0]]
        vector = jnp.concatenate(vector).reshape(-1, 128)
        vector = vector + send(vector, "weight")
        bit = 1
        while bit < nc:
            vector = vector + send(vector, "ctx", bit)
            bit *= 2
        vector = vector.reshape(-1)
        rows = vector[: 6 * width].reshape(2, 3, width)
        heads_at = 6 * width + hidden
        return (
            layer_out[None],
            grad_input[None],
            jnp.stack([grad_wq, grad_wkv[:, :cols], grad_wkv[:, cols:]], axis=1),
            grad_w_out,
            grad_w_up,
            grad_w_down,
            vector[heads_at:].reshape(2, cols),
            vector[6 * width : heads_at],
            rows[:, 0],
            rows[:, 1],
            rows[:, 2],
        )

    return local


def solution(mesh):
    return jax.shard_map(
        build(mesh.shape["weight"], mesh.shape["ctx"], mesh.shape["tensor"]),
        mesh=mesh,
        in_specs=(
            P("weight", "ctx", None),
            P("weight", None, "tensor"),
            P("weight", "tensor"),
            P("weight", "tensor"),
            P("weight", "tensor"),
            P(None, "tensor"),
            P("tensor"),
            P(),
            P(),
            P(),
            P("weight", "ctx", None),
        ),
        out_specs=(
            P("weight", "ctx", None),
            P("weight", "ctx", None),
            P(("weight", "ctx"), None, "tensor"),
            P(("weight", "ctx"), "tensor"),
            P(("weight", "ctx"), "tensor"),
            P(("weight", "ctx"), "tensor"),
            P(None, "tensor"),
            P("tensor"),
            P(),
            P(),
            P(),
        ),
        check_vma=False,
    )
```

```python
import math

import jax
import jax.numpy as jnp
from jax import lax
from jax.experimental import pallas as pl
from jax.experimental.pallas import tpu as pltpu
from jax.sharding import PartitionSpec as P


HD = 64
ROOM = pltpu.CompilerParams(vmem_limit_bytes=20 << 20)
BF = jnp.bfloat16
F32 = jnp.float32


norm_epsilon = 1e-05
inv_root_two = 1.0 / math.sqrt(2.0)
inv_root_tau = 1.0 / math.sqrt(2.0 * math.pi)

NT = (((1,), (1,)), ((), ()))
NN = (((1,), (0,)), ((), ()))
TN = (((0,), (0,)), ((), ()))


def dot(a, b, dims):
    return lax.dot_general(a, b, dims, preferred_element_type=F32)


def layer_stats(hidden):
    mean_row = jnp.mean(hidden, axis=-1, keepdims=True)
    centred = hidden - mean_row
    inverse_spread = lax.rsqrt(jnp.mean(centred * centred, axis=-1, keepdims=True) + norm_epsilon)
    return (centred * inverse_spread, inverse_spread)


def layer_back(grad_norm, normed, inverse_spread):
    return inverse_spread * (
        grad_norm
        - jnp.mean(grad_norm, axis=-1, keepdims=True)
        - normed * jnp.mean(grad_norm * normed, axis=-1, keepdims=True)
    )


def gelu_value(pre_act):
    return 0.5 * pre_act * (1.0 + lax.erf(pre_act * inv_root_two))


def gelu_slope(pre_act):
    return (
        0.5 * (1.0 + lax.erf(pre_act * inv_root_two))
        + pre_act * jnp.exp(-0.5 * pre_act * pre_act) * inv_root_tau
    )


def head_mask(shape, head):
    lane = lax.broadcasted_iota(jnp.int32, shape, 1)
    return (lane >= head * HD) & (lane < (head + 1) * HD)


def as_rows(columns, rows):
    tokens = columns[0].shape[0]
    lane = lax.broadcasted_iota(jnp.int32, (tokens, 128), 1)
    tile = jnp.zeros((tokens, 128), F32)
    for i, col in enumerate(columns):
        tile = jnp.where(lane == i, col, tile)
    return tile.T[:rows]


def attend_kernel(n, heads, *refs):
    q_ref, near_ref, far_ref = refs[:3]
    k_refs, v_refs = refs[3 : 3 + n], refs[3 + n : 3 + 2 * n]
    out_ref, lse_ref, keep_ref, sent_ref = refs[3 + 2 * n :]
    q = q_ref[...]
    out = jnp.zeros(q.shape, F32)
    lses = []
    for h in range(heads):
        mask = head_mask(q.shape, h)
        qh = jnp.where(mask, q, jnp.zeros_like(q))
        scores = [dot(qh, k[...], NT) for k in k_refs]
        top = scores[0]
        for s in scores[1:]:
            top = jnp.maximum(top, s)
        top = jnp.max(top, axis=1, keepdims=True)
        total = jnp.zeros(top.shape, F32)
        acc = jnp.zeros(q.shape, F32)
        psum = None
        for s, v in zip(scores, v_refs):
            p = jnp.exp(s - top)
            psum = p if psum is None else psum + p
            acc = acc + dot(p.astype(BF), v[...], NN)
        total = jnp.sum(psum, axis=1, keepdims=True)
        out = jnp.where(mask, acc / total, out)
        lses.append(top + jnp.log(total))
    out_ref[...] = out.astype(BF)
    lse_ref[...] = as_rows(lses, heads)
    weight = pl.ds(near_ref.shape[1] - q.shape[1], q.shape[1])
    out_kernel(out_ref, near_ref.at[:, weight], far_ref.at[:, weight], keep_ref, sent_ref)


def attend(q, near, far, ks, vs):
    n, (tokens, cols) = len(ks), q.shape
    width = 2 * near.shape[0]
    heads = cols // HD
    keys = n * tokens
    return pl.pallas_call(
        lambda *r: attend_kernel(n, heads, *r),
        out_shape=(
            jax.ShapeDtypeStruct((tokens, cols), BF),
            jax.ShapeDtypeStruct((heads, tokens), F32),
            jax.ShapeDtypeStruct((tokens // 2, width), F32),
            jax.ShapeDtypeStruct((tokens // 2, width), BF),
        ),
        cost_estimate=pl.CostEstimate(
            flops=4 * tokens * keys * cols * heads,
            bytes_accessed=2 * (2 * keys + 2 * tokens) * cols,
            transcendentals=tokens * keys * heads,
        ),
        name="attend",
        compiler_params=ROOM,
    )(q, near, far, *ks, *vs)


def split_rows(rows):
    high = rows.astype(BF)
    rest = rows - high.astype(F32)
    middle = rest.astype(BF)
    low = (rest - middle.astype(F32)).astype(BF)
    return [high, middle, low]


def message_rows(tokens, heads):
    return tokens + -(-6 * heads // 16) * 16


def pack_kernel(heads, own_ref, got_ref, near_ref, far_ref, at_ref, lse_ref, msg_ref, high_ref):
    half = near_ref.shape[0]
    one = jnp.concatenate([own_ref[...], got_ref[...]], axis=0)
    high_ref[...] = one[:, half:]
    cols = at_ref.shape[1]
    out = pl.ds(near_ref.shape[1] - cols, cols)
    da = dot(one[:, :half], near_ref[:, out], NN) + dot(one[:, half:], far_ref[:, out], NN)
    da = da.astype(BF)
    tokens = da.shape[0]
    prod = da.astype(F32) * at_ref[...].astype(F32)
    deltas = []
    for h in range(heads):
        mask = head_mask(da.shape, h)
        deltas.append(jnp.sum(jnp.where(mask, prod, 0.0), axis=1, keepdims=True))
    rows = split_rows(lse_ref[...]) + split_rows(as_rows(deltas, heads))
    spare = msg_ref.shape[0] - tokens - 6 * heads
    if spare:
        rows.append(jnp.zeros((spare, tokens), BF))
    msg_ref[:tokens, :] = da
    msg_ref[tokens:, :] = jnp.concatenate([r.astype(F32) for r in rows], axis=0).astype(BF)


def pack_message(own, got, near, far, attended, lse):
    tokens, cols = attended.shape
    heads = cols // HD
    if tokens != cols:
        raise ValueError("message shape")
    return pl.pallas_call(
        lambda *r: pack_kernel(heads, *r),
        out_shape=(
            jax.ShapeDtypeStruct((message_rows(tokens, heads), cols), BF),
            jax.ShapeDtypeStruct((tokens, own.shape[1] // 2), BF),
        ),
        cost_estimate=pl.CostEstimate(
            flops=2 * tokens * own.shape[1] * cols,
            bytes_accessed=2 * (2 * own.size + near.size + far.size + 2 * attended.size),
            transcendentals=0,
        ),
        name="pack_message",
        compiler_params=ROOM,
    )(own, got, near, far, attended, lse)


def query_kernel(n, heads, *refs):
    q_ref, da_ref, at_ref, lse_ref = refs[:4]
    k_refs, v_refs = refs[4 : 4 + n], refs[4 + n : 4 + 2 * n]
    dq_ref, sum_ref = refs[4 + 2 * n :]
    q = q_ref[...]
    tokens = q.shape[0]
    da = da_ref[:tokens, :]
    prod = da.astype(F32) * at_ref[...].astype(F32)
    lse_pad = jnp.concatenate([lse_ref[...], jnp.zeros((128 - heads, tokens), F32)], axis=0).T
    out = jnp.zeros(q.shape, F32)
    for h in range(heads):
        mask = head_mask(q.shape, h)
        zero = jnp.zeros_like(q)
        qh, dah = jnp.where(mask, q, zero), jnp.where(mask, da, zero)
        delta = jnp.sum(jnp.where(mask, prod, 0.0), axis=1, keepdims=True)
        lse = lse_pad[:, h : h + 1]
        acc = jnp.zeros(q.shape, F32)
        for k, v in zip(k_refs, v_refs):
            p = jnp.exp(dot(qh, k[...], NT) - lse)
            ds = (p * (dot(dah, v[...], NT) - delta)).astype(BF)
            acc = acc + dot(ds, k[...], NN)
        out = jnp.where(mask, acc, out)
    out = out * (HD**-0.5)
    dq_ref[...] = out.astype(BF)
    sum_ref[...] = jnp.sum(out, axis=0, keepdims=True)


def query_grads(q, msg, attended, lse, ks, vs):
    n, (tokens, cols) = len(ks), q.shape
    heads, keys = cols // HD, len(ks) * q.shape[0]
    return pl.pallas_call(
        lambda *r: query_kernel(n, heads, *r),
        out_shape=(
            jax.ShapeDtypeStruct((tokens, cols), BF),
            jax.ShapeDtypeStruct((1, cols), F32),
        ),
        cost_estimate=pl.CostEstimate(
            flops=6 * tokens * keys * cols * heads,
            bytes_accessed=2 * (2 * keys + 4 * tokens) * cols,
            transcendentals=tokens * keys * heads,
        ),
        name="query_grads",
        compiler_params=ROOM,
    )(q, msg, attended, lse, *ks, *vs)


def key_kernel(m, n, heads, *refs):
    k_ref, v_ref = refs[:2]
    tokens, cols = k_ref.shape
    qs = [
        r.at[pl.ds(i * tokens, tokens)]
        for r in refs[2 : 2 + m]
        for i in range(r.shape[0] // tokens)
    ]
    msgs = refs[2 + m : 2 + m + n]
    out_ref, sum_ref = refs[2 + m + n :]
    k, v = k_ref[...], v_ref[...]
    stats = []
    for msg in msgs:
        rows = msg[tokens:, :].astype(F32)
        part = [rows[i * heads : (i + 1) * heads] for i in range(6)]
        stats.append((part[0] + part[1] + part[2], part[3] + part[4] + part[5]))
    dk, dv = jnp.zeros(k.shape, F32), jnp.zeros(k.shape, F32)
    for h in range(heads):
        mask = head_mask(k.shape, h)
        zero = jnp.zeros_like(k)
        kh, vh = jnp.where(mask, k, zero), jnp.where(mask, v, zero)
        dk_acc, dv_acc = jnp.zeros(k.shape, F32), jnp.zeros(k.shape, F32)
        for q, msg, (lse, delta) in zip(qs, msgs, stats):
            da = msg[:tokens, :]
            p = jnp.exp(dot(kh, q[...], NT) - lse[h : h + 1, :])
            dv_acc = dv_acc + dot(p.astype(BF), da, NN)
            ds = (p * (dot(vh, da, NT) - delta[h : h + 1, :])).astype(BF)
            dk_acc = dk_acc + dot(ds, q[...], NN)
        dk, dv = jnp.where(mask, dk_acc, dk), jnp.where(mask, dv_acc, dv)
    out_ref[:, :cols] = dk.astype(BF)
    out_ref[:, cols:] = dv.astype(BF)
    sum_ref[...] = jnp.sum(dv, axis=0, keepdims=True)


def key_grads(k, v, qs, msgs):
    m, n, (tokens, cols) = len(qs), len(msgs), k.shape
    heads, rows = cols // HD, n * tokens
    return pl.pallas_call(
        lambda *r: key_kernel(m, n, heads, *r),
        out_shape=(
            jax.ShapeDtypeStruct((tokens, 2 * cols), BF),
            jax.ShapeDtypeStruct((1, cols), F32),
        ),
        cost_estimate=pl.CostEstimate(
            flops=8 * tokens * rows * cols * heads,
            bytes_accessed=2 * (2 * rows + 4 * tokens) * cols,
            transcendentals=tokens * rows * heads,
        ),
        name="key_grads",
        compiler_params=ROOM,
    )(k, v, *qs, *msgs)


def arr(rows, cols, dtype):
    return jax.ShapeDtypeStruct((rows, cols), dtype)


def call(kernel, outs, *args, flops=0, scalars=0):
    outs_list = outs if isinstance(outs, (tuple, list)) else (outs,)
    total = sum(math.prod(a.shape) * a.dtype.itemsize for a in list(args) + list(outs_list))
    return pl.pallas_call(
        kernel,
        out_shape=outs,
        in_specs=[
            pl.BlockSpec(memory_space=pltpu.SMEM if i < scalars else pltpu.VMEM)
            for i in range(len(args))
        ],
        cost_estimate=pl.CostEstimate(flops=flops, bytes_accessed=total, transcendentals=0),
        compiler_params=ROOM,
    )(*args)


def column_blocks(cols):
    size = 256 if cols % 256 == 0 else cols
    return [pl.ds(i, size) for i in range(0, cols, size)]


def put_partial(block, value, keep_ref, sent_ref):
    half = keep_ref.shape[0]
    keep_ref[:, block] = value[:half]
    sent_ref[:, block] = value[half:].astype(BF)


def out_kernel(at_ref, near_ref, far_ref, keep_ref, sent_ref):
    at = at_ref[...]
    half = near_ref.shape[0]
    for start, ref in ((0, near_ref), (half, far_ref)):
        for rows in column_blocks(half):
            value = dot(at, ref[rows, :], NT)
            put_partial(pl.ds(start + rows.start, rows.size), value, keep_ref, sent_ref)


def norm_one_kernel(sent_ref, got_ref, x_ref, bias_ref, gain_ref, shift_ref, *outs):
    mixed_ref, normed_ref, inverse_ref, own_ref = outs
    summed = sent_ref[...].astype(F32) + got_ref[...].astype(F32)
    hidden = x_ref[...].astype(F32) + summed + bias_ref[0:1, :]
    normed, inverse = layer_stats(hidden)
    mixed = normed * gain_ref[0:1, :] + shift_ref[0:1, :]
    mixed_ref[...] = mixed
    normed_ref[...] = normed
    inverse_ref[...] = jnp.broadcast_to(inverse, inverse_ref.shape)
    own_ref[...] = mixed.astype(BF)


def up_kernel(own_ref, got_ref, x_ref, at_ref, near_ref, far_ref, bias_ref, *outs):
    pre_ref, act_ref, bundle_ref = outs
    half = near_ref.shape[0]
    mixed = jnp.concatenate([own_ref[...], got_ref[...]], axis=0)
    low, high = mixed[:, :half], mixed[:, half:]
    bundle_ref[:, :half] = high
    bundle_ref[:, pl.ds(half, half)] = x_ref[:, pl.ds(half, half)]
    bundle_ref[:, pl.ds(2 * half, at_ref.shape[1])] = at_ref[...]
    for block in column_blocks(near_ref.shape[1]):
        pre = dot(low, near_ref[:, block], NN) + dot(high, far_ref[:, block], NN)
        pre = pre + bias_ref[:, block]
        pre_ref[:, block] = pre
        act_ref[:, block] = gelu_value(pre).astype(BF)


def offsets(n):
    held = [0]
    for bit in levels(n):
        held = held + [i ^ bit for i in held]
    return held


def down_kernel(rank_ref, act_ref, near_ref, *refs):
    pieces, (far_ref, keep_ref, sent_ref) = refs[:-3], refs[-3:]
    rows = pieces[0].shape[0]
    for offset, piece in zip(offsets(len(pieces)), pieces):
        at = pl.multiple_of(jnp.bitwise_xor(rank_ref[0], offset) * rows, rows)
        far_ref[pl.ds(at, rows), :] = piece[...]
    out_kernel(act_ref, near_ref, far_ref, keep_ref, sent_ref)


def norm_two_kernel(
    sent_ref, got_ref, mixed_ref, cot_ref, bias_ref, gain_ref, shift_ref, pair_ref, grad_ref, sum_ref
):
    summed = sent_ref[...].astype(F32) + got_ref[...].astype(F32)
    normed, inverse = layer_stats(mixed_ref[...] + summed + bias_ref[1:2, :])
    gain = gain_ref[1:2, :]
    cot = cot_ref[...].astype(F32)
    grad = layer_back(cot * gain, normed, inverse)
    half = grad.shape[0]
    pair_ref[:half, :] = grad.astype(BF)
    pair_ref[half:, :] = (normed * gain + shift_ref[1:2, :]).astype(BF)
    grad_ref[...] = grad
    sum_ref[0:1, :] = jnp.sum(grad, axis=0, keepdims=True)
    sum_ref[1:2, :] = jnp.sum(cot * normed, axis=0, keepdims=True)
    sum_ref[2:3, :] = jnp.sum(cot, axis=0, keepdims=True)


def back_kernel(own_ref, got_ref, dn_ref, df_ref, pre_ref, un_ref, uf_ref, *outs):
    grad_ref, sum_ref, keep_ref, sent_ref = outs
    half = dn_ref.shape[0]
    tokens = own_ref.shape[0] // 2
    two = jnp.concatenate([own_ref[:tokens, :], got_ref[:tokens, :]], axis=0)
    low, high = two[:, :half], two[:, half:]
    for block in column_blocks(dn_ref.shape[1]):
        grad = dot(low, dn_ref[:, block], NN) + dot(high, df_ref[:, block], NN)
        grad = grad * gelu_slope(pre_ref[:, block])
        sum_ref[:, block] = jnp.sum(grad, axis=0, keepdims=True)
        grad_ref[:, block] = grad.astype(BF)
    out_kernel(grad_ref, un_ref, uf_ref, keep_ref, sent_ref)


def norm_back_kernel(
    sent_ref, got_ref, two_ref, normed_ref, inverse_ref, gain_ref, sums_ref, *outs
):
    own_ref, grad_ref, sum_ref = outs
    normed = normed_ref[...]
    mixed = two_ref[...] + (sent_ref[...].astype(F32) + got_ref[...].astype(F32))
    grad = layer_back(mixed * gain_ref[0:1, :], normed, inverse_ref[:, 0:1])
    own_ref[...] = grad.astype(BF)
    grad_ref[...] = grad
    for i, value in enumerate((grad, mixed * normed, mixed)):
        sum_ref[2 * i : 2 * i + 1, :] = jnp.sum(value, axis=0, keepdims=True)
        sum_ref[2 * i + 1 : 2 * i + 2, :] = sums_ref[i : i + 1, :]


def sums_kernel(flag_ref, own_ref, got_ref, up_ref, q_ref, v_ref, out_ref):
    half, cols = own_ref.shape[1] // 2, q_ref.shape[1]
    rows = own_ref[...] + got_ref[...]
    turned = jnp.concatenate([rows[:, half:], rows[:, :half]], axis=1)
    out_ref[0:6, :] = jnp.where(flag_ref[0] == 1, turned, rows)
    out_ref[6:7, :] = up_ref[...]
    out_ref[7:8, :] = jnp.zeros((1, 2 * half), F32)
    out_ref[7:8, pl.ds(0, cols)] = q_ref[...]
    out_ref[7:8, pl.ds(cols, cols)] = v_ref[...]


def unpack_kernel(a_ref, b_ref, head_ref, up_ref, bias_ref, gain_ref, shift_ref):
    total = a_ref[...] + b_ref[...]
    cols = head_ref.shape[1]
    bias_ref[...] = total[0:2]
    gain_ref[...] = total[2:4]
    shift_ref[...] = total[4:6]
    up_ref[...] = total[6:7]
    head_ref[0:1, :] = total[7:8, :cols]
    head_ref[1:2, :] = total[7:8, cols : 2 * cols]


def input_kernel(dq_ref, dkv_ref, *refs):
    near, far, (keep_ref, sent_ref) = refs[:3], refs[3:6], refs[6:]
    dq = dq_ref[...]
    cols, half = dq.shape[1], near[0].shape[0]
    dk, dv = dkv_ref[:, :cols], dkv_ref[:, cols:]
    for start, (q_ref, k_ref, v_ref) in ((0, near), (half, far)):
        for rows in column_blocks(half):
            value = dot(dq, q_ref[rows, pl.ds(0, cols)], NT)
            value = value + dot(dk, k_ref[rows, :], NT) + dot(dv, v_ref[rows, :], NT)
            put_partial(pl.ds(start + rows.start, rows.size), value, keep_ref, sent_ref)


def weight_kernel(n, terms, mine_ref, *refs):
    ins, (away_ref, stay_ref) = refs[:-2], refs[-2:]
    rows = away_ref.shape[1]
    mine = mine_ref[0]
    for i in range(n // 2):
        for out, side in ((away_ref, 1 - mine), (stay_ref, mine)):
            at = (2 * i + side) * rows
            col = 0
            for group in terms:
                value = None
                for pieces, low, b in group:
                    block = pl.ds(pl.multiple_of(at + low, 128), rows)
                    a = [ins[k][pl.ds(0, count), block] for k, count in pieces]
                    a = a[0] if len(a) == 1 else jnp.concatenate(a, axis=0)
                    where, first, cols = b
                    term = dot(a, ins[where][:, pl.ds(first, cols)], TN)
                    value = term if value is None else value + term
                out[i, :, pl.ds(col, value.shape[1])] = value.astype(BF)
                col += value.shape[1]


def levels(n):
    return [1 << i for i in reversed(range(n.bit_length() - 1))]


def build(nw, nc, nt):
    if nw != 2 or nt % 2 or nc & (nc - 1) or nt & (nt - 1):
        raise ValueError("mesh")
    sizes = {"weight": nw, "ctx": nc, "tensor": nt}

    def send(a, axis, bit=1):
        return lax.ppermute(a, axis, [(i, i ^ bit) for i in range(sizes[axis])])

    def settle(keep, sent):
        total = keep + send(sent, "tensor").astype(F32)
        bit = 2
        while bit < nt:
            sent = total.astype(BF)
            got = send(sent, "tensor", bit)
            total = sent.astype(F32) + got.astype(F32)
            bit *= 2
        return sent, got

    def gather(a):
        held, bit = [a], nc // 2
        while bit:
            held = held + [send(h, "ctx", bit) for h in held]
            bit //= 2
        return held

    def gather_few(a):
        held, bit = [a], nc // 2
        while bit:
            whole = held[0] if len(held) == 1 else jnp.concatenate(held, axis=0)
            held = held + [send(whole, "ctx", bit)]
            bit //= 2
        return held

    def owned(products, after, bits, mines):
        rows = products[0][0][3] // nc
        cols = sum(p[0][2][2] for p in products)
        if rows % 128 == 0:
            flat, terms, flops = [], [], 0
            for group in products:
                terms.append([])
                for stack, low, (b, first, wide), high in group:
                    pieces = [(len(flat) + i, count) for i, (_, count) in enumerate(stack)]
                    flat += [ref for ref, _ in stack] + [b]
                    terms[-1].append((pieces, low, (len(flat) - 1, first, wide)))
                    flops += 2 * b.shape[0] * high * wide
            part = jax.ShapeDtypeStruct((nc // 2, rows, cols), BF)
            away, stay = call(
                lambda *r: weight_kernel(nc, terms, *r),
                (part, part),
                mines,
                *flat,
                flops=flops,
                scalars=1,
            )
        else:
            grad = []
            for group in products:
                value = 0.0
                for stack, low, (b, first, wide), high in group:
                    lhs = jnp.concatenate([r[:c, low : low + high] for r, c in stack], axis=0)
                    value = value + dot(lhs, b[:, first : first + wide], TN)
                grad.append(value.astype(BF))
            view = jnp.concatenate(grad, axis=1).reshape(nc // 2, 2, rows, cols)
            away = jnp.where(bits[0], view[:, 0], view[:, 1])
            stay = jnp.where(bits[0], view[:, 1], view[:, 0])
        bit = 1
        while True:
            got = send(away, "ctx", bit)
            got, stay, _ = lax.optimization_barrier((got, stay, after[0]))
            after = after[1:]
            total = stay.astype(F32) + got.astype(F32)
            bit *= 2
            if bit == nc:
                return total.reshape(rows, cols)
            view = total.reshape(total.shape[0] // 2, 2, rows, cols)
            upper = bits[bit.bit_length() - 1]
            away = jnp.where(upper, view[:, 0], view[:, 1]).astype(BF)
            stay = jnp.where(upper, view[:, 1], view[:, 0])

    def local(
        inputs, w_qkv, w_out, w_up, w_down, head_bias, up_bias, out_biases,
        norm_gains, norm_shifts, cotangent,
    ):
        tokens, width = inputs.shape[1], inputs.shape[2]
        half_t, half_d = tokens // 2, width // 2
        cols, hidden = w_qkv.shape[2], w_up.shape[1]
        rank = lax.axis_index("ctx")
        bits = [jnp.bitwise_and(rank, bit) != 0 for bit in reversed(levels(nc))]
        piece_at = rank * (half_d // nc)
        far_weight = lax.axis_index("weight") == 1
        far_core = jnp.bitwise_and(lax.axis_index("tensor"), 1) == 1
        ranks = rank.reshape(1)
        mines = jnp.bitwise_and(ranks, 1)
        flags = far_weight.astype(jnp.int32).reshape(1)
        early = (piece_at, far_weight, far_core, ranks, mines, flags, *bits)
        (inputs, w_qkv, w_out, w_up, w_down, cotangent), early = lax.optimization_barrier(
            ((inputs, w_qkv, w_out, w_up, w_down, cotangent), early)
        )
        piece_at, far_weight, far_core, ranks, mines, flags = early[:6]
        bits = early[6:]

        def turn_d(a):
            return jnp.where(far_weight, jnp.concatenate([a[:, half_d:], a[:, :half_d]], 1), a)

        def turn_t(a):
            return jnp.where(far_core, jnp.concatenate([a[half_t:], a[:half_t]], 0), a)

        wq, wk, wv = w_qkv[:, 0], w_qkv[:, 1], w_qkv[:, 2]
        wqo = jnp.concatenate([wq, w_out], axis=1)
        wk_far = send(wk, "weight")
        wv_far = send(wv, "weight")
        wqo_far = send(wqo, "weight")
        piece = lax.dynamic_slice_in_dim(w_down, piece_at, half_d // nc, 0)
        piece = send(piece, "weight")
        up_far = send(w_up, "weight")
        pieces = gather(piece)

        x = turn_t(turn_d(inputs[0]))
        x_own = x[:half_t]
        cot = turn_t(turn_d(cotangent[0]))[:half_t]
        out_b, gains, shifts = turn_d(out_biases), turn_d(norm_gains), turn_d(norm_shifts)
        x_lo, x_hi = x[:, :half_d], x[:, half_d:]

        k = (dot(x_lo, wk, NN) + dot(x_hi, wk_far, NN)).astype(BF)
        ks = gather(k)
        v = (dot(x_lo, wv, NN) + dot(x_hi, wv_far, NN) + head_bias[1]).astype(BF)
        vs = gather(v)
        q = dot(x_lo, wq, NN) + dot(x_hi, wqo_far[:, :cols], NN) + head_bias[0]
        q = q.astype(BF) * BF(HD**-0.5)
        qs = gather_few(q)

        part = (arr(half_t, width, F32), arr(half_t, width, BF))
        attended, lse, keep, sent = attend(q, wqo, wqo_far, ks, vs)
        sent, got = settle(keep, sent)
        mixed_one, normed_one, inverse_one, mixed_own = call(
            norm_one_kernel,
            (part[0], part[0], arr(half_t, 128, F32), part[1]),
            sent, got, x_own, out_b, gains, shifts,
        )
        mixed_got = send(mixed_own, "tensor")
        big = 2 * tokens * width * hidden
        pre_act, act, bundle = call(
            up_kernel,
            (arr(tokens, hidden, F32), arr(tokens, hidden, BF), arr(tokens, width + cols, BF)),
            mixed_own, mixed_got, x, attended, w_up, up_far, up_bias.reshape(1, hidden),
            flops=big,
        )
        bundle = send(bundle, "weight")
        down_far, keep, sent = call(
            down_kernel,
            (arr(half_d, hidden, BF),) + part,
            ranks, act, w_down, *pieces,
            flops=big, scalars=1,
        )
        sent, got = settle(keep, sent)
        act_mate = send(act, "weight")
        pair, grad_two, sums_two = call(
            norm_two_kernel,
            (arr(tokens, width, BF), part[0], arr(3, width, F32)),
            sent, got, mixed_one, cot, out_b, gains, shifts,
        )
        pair_got = send(pair, "tensor")
        two_hi = jnp.concatenate([pair[:half_t, half_d:], pair_got[:half_t, half_d:]], axis=0)
        two_mate = send(two_hi, "weight")
        grad_pre, grad_up_b, keep, sent = call(
            back_kernel,
            (arr(tokens, hidden, BF), arr(1, hidden, F32)) + part,
            pair, pair_got, w_down, down_far, pre_act, w_up, up_far,
            flops=2 * big,
        )
        sent, got = settle(keep, sent)
        pre_mate = send(grad_pre, "weight")
        one_own, grad_one, sums_one = call(
            norm_back_kernel,
            (part[1], part[0], arr(6, width, F32)),
            sent, got, grad_two, normed_one, inverse_one, gains, sums_two,
        )
        one_got = send(one_own, "tensor")
        msg, one_hi = pack_message(one_own, one_got, wqo, wqo_far, attended, lse)
        msgs = gather(msg)
        one_mate = send(one_hi, "weight")
        dq, sums_q = query_grads(q, msg, attended, lse, ks, vs)
        dq_mate = send(dq, "weight")
        dkv, sums_v = key_grads(k, v, qs, msgs)

        dkv_mate = send(dkv, "weight")
        keep, sent = call(
            input_kernel, part, dq, dkv, wqo, wk, wv, wqo_far, wk_far, wv_far,
            flops=6 * tokens * width * cols,
        )
        late = [sent] * 8

        def term(stack, b, low=0, first=0, wide=None):
            return ([(r, r.shape[0] if c is None else c) for r, c in stack], low,
                    (b, first, b.shape[1] if wide is None else wide), half_d)

        grad_w_down = owned(
            [[term([(pair, half_t), (pair_got, half_t)], act), term([(two_mate, None)], act_mate)]],
            [dq] + late,
            bits,
            mines,
        )
        grad_w_up = owned(
            [[
                term([(mixed_own, None), (mixed_got, None)], grad_pre),
                term([(bundle, None)], pre_mate),
            ]],
            late,
            bits,
            mines,
        )
        oq_grad = owned(
            [
                [
                    term([(one_own, None), (one_got, None)], attended),
                    term([(one_mate, None)], bundle, first=width, wide=cols),
                ],
                [term([(x, None)], dq), term([(bundle, None)], dq_mate, low=half_d)],
            ],
            late,
            bits,
            mines,
        )
        grad_w_out, grad_wq = oq_grad[:, :cols], oq_grad[:, cols:]
        sent, got = settle(keep, sent)
        grad_wkv = owned(
            [[term([(x, None)], dkv), term([(bundle, None)], dkv_mate, low=half_d)]],
            late,
            bits,
            mines,
        )
        grad_own = (grad_one + (sent.astype(F32) + got.astype(F32))).astype(BF)
        grad_got = send(grad_own, "tensor")
        grad_input = turn_d(turn_t(jnp.concatenate([grad_own, grad_got], axis=0)))
        pair, pair_got, _ = lax.optimization_barrier((pair, pair_got, late[0]))
        layer_out = turn_d(turn_t(jnp.concatenate([pair[half_t:], pair_got[half_t:]], axis=0)))

        if hidden != width or 2 * cols > width:
            raise ValueError("vector shape")
        sums_got = send(sums_one, "tensor")
        vector = call(
            sums_kernel, arr(8, width, F32),
            flags, sums_one, sums_got, grad_up_b, sums_q, sums_v, scalars=1,
        )
        got = send(vector, "weight")
        bit = 1
        while bit < nc:
            vector = vector + got
            got = send(vector, "ctx", bit)
            bit *= 2
        head, up_row, bias, gain, shift = call(
            unpack_kernel,
            (arr(2, cols, F32), arr(1, hidden, F32)) + (arr(2, width, F32),) * 3,
            vector, got,
        )
        return (
            layer_out[None],
            grad_input[None],
            jnp.stack([grad_wq, grad_wkv[:, :cols], grad_wkv[:, cols:]], axis=1),
            grad_w_out,
            grad_w_up,
            grad_w_down,
            head,
            up_row[0],
            bias,
            gain,
            shift,
        )

    return local


def solution(mesh):
    return jax.shard_map(
        build(mesh.shape["weight"], mesh.shape["ctx"], mesh.shape["tensor"]),
        mesh=mesh,
        in_specs=(
            P("weight", "ctx", None),
            P("weight", None, "tensor"),
            P("weight", "tensor"),
            P("weight", "tensor"),
            P("weight", "tensor"),
            P(None, "tensor"),
            P("tensor"),
            P(),
            P(),
            P(),
            P("weight", "ctx", None),
        ),
        out_specs=(
            P("weight", "ctx", None),
            P("weight", "ctx", None),
            P(("weight", "ctx"), None, "tensor"),
            P(("weight", "ctx"), "tensor"),
            P(("weight", "ctx"), "tensor"),
            P(("weight", "ctx"), "tensor"),
            P(None, "tensor"),
            P("tensor"),
            P(),
            P(),
            P(),
        ),
        check_vma=False,
    )
```

```python
import math

import jax
import jax.numpy as jnp
from jax import lax
from jax.experimental import pallas as pl
from jax.experimental.pallas import tpu as pltpu
from jax.sharding import PartitionSpec as P


HD = 64
ROOM = pltpu.CompilerParams(vmem_limit_bytes=20 << 20)
BF = jnp.bfloat16
F32 = jnp.float32


norm_epsilon = 1e-05
inv_root_two = 1.0 / math.sqrt(2.0)
inv_root_tau = 1.0 / math.sqrt(2.0 * math.pi)

NT = (((1,), (1,)), ((), ()))
NN = (((1,), (0,)), ((), ()))
TN = (((0,), (0,)), ((), ()))


def dot(a, b, dims):
    return lax.dot_general(a, b, dims, preferred_element_type=F32)


def layer_stats(hidden):
    mean_row = jnp.mean(hidden, axis=-1, keepdims=True)
    centred = hidden - mean_row
    inverse_spread = lax.rsqrt(jnp.mean(centred * centred, axis=-1, keepdims=True) + norm_epsilon)
    return (centred * inverse_spread, inverse_spread)


def layer_back(grad_norm, normed, inverse_spread):
    return inverse_spread * (
        grad_norm
        - jnp.mean(grad_norm, axis=-1, keepdims=True)
        - normed * jnp.mean(grad_norm * normed, axis=-1, keepdims=True)
    )


def gelu_value(pre_act):
    return 0.5 * pre_act * (1.0 + lax.erf(pre_act * inv_root_two))


def gelu_slope(pre_act):
    return (
        0.5 * (1.0 + lax.erf(pre_act * inv_root_two))
        + pre_act * jnp.exp(-0.5 * pre_act * pre_act) * inv_root_tau
    )


def head_mask(shape, head):
    lane = lax.broadcasted_iota(jnp.int32, shape, 1)
    return (lane >= head * HD) & (lane < (head + 1) * HD)


def as_rows(columns, rows):
    tokens = columns[0].shape[0]
    lane = lax.broadcasted_iota(jnp.int32, (tokens, 128), 1)
    tile = jnp.zeros((tokens, 128), F32)
    for i, col in enumerate(columns):
        tile = jnp.where(lane == i, col, tile)
    return tile.T[:rows]


def attend_kernel(n, heads, *refs):
    q_ref, near_ref, far_ref = refs[:3]
    k_refs, v_refs = refs[3 : 3 + n], refs[3 + n : 3 + 2 * n]
    out_ref, lse_ref, keep_ref, sent_ref = refs[3 + 2 * n :]
    q = q_ref[...]
    out = jnp.zeros(q.shape, F32)
    lses = []
    for h in range(heads):
        mask = head_mask(q.shape, h)
        qh = jnp.where(mask, q, jnp.zeros_like(q))
        scores = [dot(qh, k[...], NT) for k in k_refs]
        top = scores[0]
        for s in scores[1:]:
            top = jnp.maximum(top, s)
        top = jnp.max(top, axis=1, keepdims=True)
        total = jnp.zeros(top.shape, F32)
        acc = jnp.zeros(q.shape, F32)
        psum = None
        for s, v in zip(scores, v_refs):
            p = jnp.exp(s - top)
            psum = p if psum is None else psum + p
            acc = acc + dot(p.astype(BF), v[...], NN)
        total = jnp.sum(psum, axis=1, keepdims=True)
        out = jnp.where(mask, acc / total, out)
        lses.append(top + jnp.log(total))
    out_ref[...] = out.astype(BF)
    lse_ref[...] = as_rows(lses, heads)
    weight = pl.ds(near_ref.shape[1] - q.shape[1], q.shape[1])
    out_kernel(out_ref, near_ref.at[:, weight], far_ref.at[:, weight], keep_ref, sent_ref)


def attend(q, near, far, ks, vs):
    n, (tokens, cols) = len(ks), q.shape
    width = 2 * near.shape[0]
    heads = cols // HD
    keys = n * tokens
    return pl.pallas_call(
        lambda *r: attend_kernel(n, heads, *r),
        out_shape=(
            jax.ShapeDtypeStruct((tokens, cols), BF),
            jax.ShapeDtypeStruct((heads, tokens), F32),
            jax.ShapeDtypeStruct((tokens // 2, width), F32),
            jax.ShapeDtypeStruct((tokens // 2, width), BF),
        ),
        cost_estimate=pl.CostEstimate(
            flops=4 * tokens * keys * cols * heads,
            bytes_accessed=2 * (2 * keys + 2 * tokens) * cols,
            transcendentals=tokens * keys * heads,
        ),
        name="attend",
        compiler_params=ROOM,
    )(q, near, far, *ks, *vs)


def split_rows(rows):
    high = rows.astype(BF)
    rest = rows - high.astype(F32)
    middle = rest.astype(BF)
    low = (rest - middle.astype(F32)).astype(BF)
    return [high, middle, low]


def join_rows(parts, count):
    wide = parts.astype(F32)
    return wide[:count] + wide[count : 2 * count] + wide[2 * count : 3 * count]


def stack_rows(parts, rows):
    parts = [p.astype(F32) for p in parts]
    spare = rows - sum(p.shape[0] for p in parts)
    if spare:
        parts.append(jnp.zeros((spare, parts[0].shape[1]), F32))
    return jnp.concatenate(parts, axis=0).astype(BF)


def folded(rows, cols):
    return jnp.concatenate([rows[:, i : i + cols] for i in range(0, rows.shape[1], cols)], axis=0)


def unfolded(rows, count):
    return jnp.concatenate(
        [rows[i : i + count] for i in range(0, rows.shape[0], count)], axis=1
    )


def settled_rows(rows):
    high, middle, low = split_rows(rows)
    return high.astype(F32) + middle.astype(F32) + low.astype(F32)


def message_rows(tokens, heads):
    return tokens + -(-6 * heads // 16) * 16


def pack_kernel(
    heads, flag_ref, own_ref, got_ref, near_ref, far_ref, at_ref, lse_ref, x_ref, up_ref, *outs
):
    msg_ref, bundle_ref, vector_ref = outs
    half = near_ref.shape[0]
    tokens, cols = at_ref.shape
    part = tokens // 2
    one = jnp.concatenate([own_ref[:part, :], got_ref[:part, :]], axis=0)
    bundle_ref[:tokens, :half] = one[:, half:]
    bundle_ref[:tokens, pl.ds(half, half)] = x_ref[:, pl.ds(half, half)]
    bundle_ref[:tokens, pl.ds(2 * half, cols)] = at_ref[...]
    out = pl.ds(near_ref.shape[1] - cols, cols)
    da = dot(one[:, :half], near_ref[:, out], NN) + dot(one[:, half:], far_ref[:, out], NN)
    da = da.astype(BF)
    rows = join_rows(own_ref[part:, :], 6) + join_rows(got_ref[part:, :], 6)
    turned = jnp.concatenate([rows[:, half:], rows[:, :half]], axis=1)
    vector_ref[0:6, :] = jnp.where(flag_ref[0] == 1, turned, rows)
    vector_ref[6:7, :] = up_ref[...]
    vector_ref[7:8, :] = jnp.zeros((1, 2 * half), F32)
    vector_ref[7:8, pl.ds(cols, cols)] = jnp.sum(da.astype(F32), axis=0, keepdims=True)
    extra = bundle_ref.shape[0] - tokens
    bundle_ref[tokens:, : 2 * half] = stack_rows(split_rows(vector_ref[...]), extra)
    bundle_ref[tokens:, pl.ds(2 * half, cols)] = jnp.zeros((extra, cols), BF)
    prod = da.astype(F32) * at_ref[...].astype(F32)
    deltas = []
    for h in range(heads):
        mask = head_mask(da.shape, h)
        deltas.append(jnp.sum(jnp.where(mask, prod, 0.0), axis=1, keepdims=True))
    rows = split_rows(lse_ref[...]) + split_rows(as_rows(deltas, heads))
    msg_ref[:tokens, :] = da
    msg_ref[tokens:, :] = stack_rows(rows, msg_ref.shape[0] - tokens)


def pack_message(flags, own, got, near, far, attended, lse, x, up_row):
    tokens, cols = attended.shape
    width, heads = own.shape[1], cols // HD
    if tokens != cols or up_row.shape[1] != width or 2 * cols > width:
        raise ValueError("message shape")
    return call(
        lambda *r: pack_kernel(heads, *r),
        (
            arr(message_rows(tokens, heads), cols, BF),
            arr(tokens + 32, width + cols, BF),
            arr(8, width, F32),
        ),
        flags, own, got, near, far, attended, lse, x, up_row,
        flops=2 * tokens * width * cols, scalars=1,
    )


def query_kernel(n, heads, *refs):
    q_ref, da_ref, at_ref, lse_ref = refs[:4]
    k_refs, v_refs = refs[4 : 4 + n], refs[4 + n : 4 + 2 * n]
    dq_ref = refs[4 + 2 * n]
    q = q_ref[...]
    tokens = q.shape[0]
    da = da_ref[:tokens, :]
    prod = da.astype(F32) * at_ref[...].astype(F32)
    lse_pad = jnp.concatenate([lse_ref[...], jnp.zeros((128 - heads, tokens), F32)], axis=0).T
    out = jnp.zeros(q.shape, F32)
    for h in range(heads):
        mask = head_mask(q.shape, h)
        zero = jnp.zeros_like(q)
        qh, dah = jnp.where(mask, q, zero), jnp.where(mask, da, zero)
        delta = jnp.sum(jnp.where(mask, prod, 0.0), axis=1, keepdims=True)
        lse = lse_pad[:, h : h + 1]
        acc = jnp.zeros(q.shape, F32)
        for k, v in zip(k_refs, v_refs):
            p = jnp.exp(dot(qh, k[...], NT) - lse)
            ds = (p * (dot(dah, v[...], NT) - delta)).astype(BF)
            acc = acc + dot(ds, k[...], NN)
        out = jnp.where(mask, acc, out)
    out = out * (HD**-0.5)
    dq_ref[:tokens, :] = out.astype(BF)
    sums = jnp.sum(out, axis=0, keepdims=True)
    dq_ref[tokens:, :] = stack_rows(split_rows(sums), dq_ref.shape[0] - tokens)


def query_grads(q, msg, attended, lse, ks, vs):
    n, (tokens, cols) = len(ks), q.shape
    heads, keys = cols // HD, len(ks) * q.shape[0]
    return pl.pallas_call(
        lambda *r: query_kernel(n, heads, *r),
        out_shape=jax.ShapeDtypeStruct((tokens + 16, cols), BF),
        cost_estimate=pl.CostEstimate(
            flops=6 * tokens * keys * cols * heads,
            bytes_accessed=2 * (2 * keys + 4 * tokens) * cols,
            transcendentals=tokens * keys * heads,
        ),
        name="query_grads",
        compiler_params=ROOM,
    )(q, msg, attended, lse, *ks, *vs)


def key_kernel(m, n, heads, *refs):
    k_ref, v_ref = refs[:2]
    tokens, cols = k_ref.shape
    qs = [
        r.at[pl.ds(i * tokens, tokens)]
        for r in refs[2 : 2 + m]
        for i in range(r.shape[0] // tokens)
    ]
    msgs = refs[2 + m : 2 + m + n]
    out_ref = refs[2 + m + n]
    k, v = k_ref[...], v_ref[...]
    stats = []
    for msg in msgs:
        rows = msg[tokens:, :].astype(F32)
        part = [rows[i * heads : (i + 1) * heads] for i in range(6)]
        stats.append((part[0] + part[1] + part[2], part[3] + part[4] + part[5]))
    dk, dv = jnp.zeros(k.shape, F32), jnp.zeros(k.shape, F32)
    for h in range(heads):
        mask = head_mask(k.shape, h)
        zero = jnp.zeros_like(k)
        kh, vh = jnp.where(mask, k, zero), jnp.where(mask, v, zero)
        dk_acc, dv_acc = jnp.zeros(k.shape, F32), jnp.zeros(k.shape, F32)
        for q, msg, (lse, delta) in zip(qs, msgs, stats):
            da = msg[:tokens, :]
            p = jnp.exp(dot(kh, q[...], NT) - lse[h : h + 1, :])
            dv_acc = dv_acc + dot(p.astype(BF), da, NN)
            ds = (p * (dot(vh, da, NT) - delta[h : h + 1, :])).astype(BF)
            dk_acc = dk_acc + dot(ds, q[...], NN)
        dk, dv = jnp.where(mask, dk_acc, dk), jnp.where(mask, dv_acc, dv)
    out_ref[:, :cols] = dk.astype(BF)
    out_ref[:, cols:] = dv.astype(BF)


def key_grads(k, v, qs, msgs):
    m, n, (tokens, cols) = len(qs), len(msgs), k.shape
    heads, rows = cols // HD, n * tokens
    return pl.pallas_call(
        lambda *r: key_kernel(m, n, heads, *r),
        out_shape=jax.ShapeDtypeStruct((tokens, 2 * cols), BF),
        cost_estimate=pl.CostEstimate(
            flops=8 * tokens * rows * cols * heads,
            bytes_accessed=2 * (2 * rows + 4 * tokens) * cols,
            transcendentals=tokens * rows * heads,
        ),
        name="key_grads",
        compiler_params=ROOM,
    )(k, v, *qs, *msgs)


def arr(rows, cols, dtype):
    return jax.ShapeDtypeStruct((rows, cols), dtype)


def call(kernel, outs, *args, flops=0, scalars=0):
    outs_list = outs if isinstance(outs, (tuple, list)) else (outs,)
    total = sum(math.prod(a.shape) * a.dtype.itemsize for a in list(args) + list(outs_list))
    return pl.pallas_call(
        kernel,
        out_shape=outs,
        in_specs=[
            pl.BlockSpec(memory_space=pltpu.SMEM if i < scalars else pltpu.VMEM)
            for i in range(len(args))
        ],
        cost_estimate=pl.CostEstimate(flops=flops, bytes_accessed=total, transcendentals=0),
        compiler_params=ROOM,
    )(*args)


def column_blocks(cols):
    size = 256 if cols % 256 == 0 else cols
    return [pl.ds(i, size) for i in range(0, cols, size)]


def put_partial(block, value, keep_ref, sent_ref):
    half = keep_ref.shape[0]
    keep_ref[:, block] = value[:half]
    sent_ref[:, block] = value[half:].astype(BF)


def out_kernel(at_ref, near_ref, far_ref, keep_ref, sent_ref):
    at = at_ref[...]
    half = near_ref.shape[0]
    for start, ref in ((0, near_ref), (half, far_ref)):
        for rows in column_blocks(half):
            value = dot(at, ref[rows, :], NT)
            put_partial(pl.ds(start + rows.start, rows.size), value, keep_ref, sent_ref)


def norm_one_kernel(sent_ref, got_ref, x_ref, bias_ref, gain_ref, shift_ref, *outs):
    mixed_ref, normed_ref, inverse_ref, own_ref = outs
    summed = sent_ref[...].astype(F32) + got_ref[...].astype(F32)
    hidden = x_ref[...].astype(F32) + summed + bias_ref[0:1, :]
    normed, inverse = layer_stats(hidden)
    mixed = normed * gain_ref[0:1, :] + shift_ref[0:1, :]
    mixed_ref[...] = mixed
    normed_ref[...] = normed
    inverse_ref[...] = jnp.broadcast_to(inverse, inverse_ref.shape)
    own_ref[...] = mixed.astype(BF)


def up_kernel(own_ref, got_ref, near_ref, far_ref, bias_ref, pre_ref, act_ref, high_ref):
    half = near_ref.shape[0]
    mixed = jnp.concatenate([own_ref[...], got_ref[...]], axis=0)
    low, high = mixed[:, :half], mixed[:, half:]
    high_ref[...] = high
    for block in column_blocks(near_ref.shape[1]):
        pre = dot(low, near_ref[:, block], NN) + dot(high, far_ref[:, block], NN)
        pre = pre + bias_ref[:, block]
        pre_ref[:, block] = pre
        act_ref[:, block] = gelu_value(pre).astype(BF)


def offsets(n):
    held = [0]
    for bit in levels(n):
        held = held + [i ^ bit for i in held]
    return held


def down_kernel(rank_ref, act_ref, near_ref, *refs):
    pieces, (far_ref, keep_ref, sent_ref) = refs[:-3], refs[-3:]
    rows = pieces[0].shape[0]
    for offset, piece in zip(offsets(len(pieces)), pieces):
        at = pl.multiple_of(jnp.bitwise_xor(rank_ref[0], offset) * rows, rows)
        far_ref[pl.ds(at, rows), :] = piece[...]
    out_kernel(act_ref, near_ref, far_ref, keep_ref, sent_ref)


def norm_two_kernel(
    sent_ref, got_ref, mixed_ref, cot_ref, bias_ref, gain_ref, shift_ref, pair_ref, grad_ref, sum_ref
):
    summed = sent_ref[...].astype(F32) + got_ref[...].astype(F32)
    normed, inverse = layer_stats(mixed_ref[...] + summed + bias_ref[1:2, :])
    gain = gain_ref[1:2, :]
    cot = cot_ref[...].astype(F32)
    grad = layer_back(cot * gain, normed, inverse)
    half = grad.shape[0]
    pair_ref[:half, :] = grad.astype(BF)
    pair_ref[half:, :] = (normed * gain + shift_ref[1:2, :]).astype(BF)
    grad_ref[...] = grad
    sum_ref[0:1, :] = jnp.sum(grad, axis=0, keepdims=True)
    sum_ref[1:2, :] = jnp.sum(cot * normed, axis=0, keepdims=True)
    sum_ref[2:3, :] = jnp.sum(cot, axis=0, keepdims=True)


def back_kernel(own_ref, got_ref, dn_ref, df_ref, pre_ref, un_ref, uf_ref, *outs):
    grad_ref, sum_ref, keep_ref, sent_ref = outs
    half = dn_ref.shape[0]
    tokens = own_ref.shape[0] // 2
    two = jnp.concatenate([own_ref[:tokens, :], got_ref[:tokens, :]], axis=0)
    low, high = two[:, :half], two[:, half:]
    for block in column_blocks(dn_ref.shape[1]):
        grad = dot(low, dn_ref[:, block], NN) + dot(high, df_ref[:, block], NN)
        grad = grad * gelu_slope(pre_ref[:, block])
        sum_ref[:, block] = jnp.sum(grad, axis=0, keepdims=True)
        grad_ref[:, block] = grad.astype(BF)
    out_kernel(grad_ref, un_ref, uf_ref, keep_ref, sent_ref)


def norm_back_kernel(
    sent_ref, got_ref, two_ref, normed_ref, inverse_ref, gain_ref, sums_ref, *outs
):
    own_ref, grad_ref = outs
    normed = normed_ref[...]
    mixed = two_ref[...] + (sent_ref[...].astype(F32) + got_ref[...].astype(F32))
    grad = layer_back(mixed * gain_ref[0:1, :], normed, inverse_ref[:, 0:1])
    tokens = grad.shape[0]
    own_ref[:tokens, :] = grad.astype(BF)
    grad_ref[...] = grad
    sums = []
    for i, value in enumerate((grad, mixed * normed, mixed)):
        sums += [jnp.sum(value, axis=0, keepdims=True), sums_ref[i : i + 1, :]]
    rows = own_ref.shape[0] - tokens
    own_ref[tokens:, :] = stack_rows(split_rows(jnp.concatenate(sums, axis=0)), rows)


def input_kernel(dq_ref, dkv_ref, *refs):
    near, far, (keep_ref, sent_ref) = refs[:3], refs[3:6], refs[6:]
    dq = dq_ref[: dkv_ref.shape[0], :]
    cols, half = dq.shape[1], near[0].shape[0]
    dk, dv = dkv_ref[:, :cols], dkv_ref[:, cols:]
    for start, (q_ref, k_ref, v_ref) in ((0, near), (half, far)):
        for rows in column_blocks(half):
            value = dot(dq, q_ref[rows, pl.ds(0, cols)], NT)
            value = value + dot(dk, k_ref[rows, :], NT) + dot(dv, v_ref[rows, :], NT)
            put_partial(pl.ds(start + rows.start, rows.size), value, keep_ref, sent_ref)


def weight_kernel(n, terms, rows, ride, mine_ref, *refs):
    count = 3 if ride else 2
    ins, outs = refs[:-count], refs[-count:]
    away_ref, stay_ref = outs[:2]
    mine = mine_ref[0]
    for i in range(n // 2):
        for out, side in ((away_ref, 1 - mine), (stay_ref, mine)):
            at = (2 * i + side) * rows
            col = 0
            for group in terms:
                value = None
                for pieces, low, b in group:
                    block = pl.ds(pl.multiple_of(at + low, 128), rows)
                    a = [ins[k][pl.ds(0, tall), block] for k, tall in pieces]
                    a = a[0] if len(a) == 1 else jnp.concatenate(a, axis=0)
                    where, first, cols = b
                    b = ins[where][pl.ds(0, a.shape[0]), pl.ds(first, cols)]
                    term = dot(a, b, TN)
                    value = term if value is None else value + term
                out[pl.ds(i * rows, rows), pl.ds(col, value.shape[1])] = value.astype(BF)
                col += value.shape[1]
    if ride:
        tokens, vector, bundle, dq, dq_mate = ride
        width = ins[vector].shape[1]
        rows_x = settled_rows(ins[vector][...])
        outs[2][...] = rows_x + join_rows(ins[bundle][tokens:, :width], 8)
        sums = join_rows(ins[dq][tokens:, :], 1) + join_rows(ins[dq_mate][tokens:, :], 1)
        outs[2][7:8, pl.ds(0, sums.shape[1])] = sums
        put_vector(outs[2][...], away_ref, n // 2 * rows)


def put_vector(vector, away_ref, first):
    cols = away_ref.shape[1]
    parts = [folded(p.astype(F32), cols).astype(BF) for p in split_rows(vector)]
    away_ref[first:, :] = stack_rows(parts, away_ref.shape[0] - first)


def take_vector(got_ref, first, width):
    cols = got_ref.shape[1]
    return unfolded(join_rows(got_ref[first:, :], 8 * width // cols), 8)


def middle_kernel(blocks, rows, mine_ref, stay_ref, got_ref, *refs):
    mine = mine_ref[0]
    ride = len(refs) == 4
    away_ref, kept_ref = refs[1:3] if ride else refs
    for i in range(blocks // 2):
        for out, side in ((away_ref, 1 - mine), (kept_ref, mine)):
            at = pl.ds(pl.multiple_of((2 * i + side) * rows, rows), rows)
            value = stay_ref[at, :].astype(F32) + got_ref[at, :].astype(F32)
            out[pl.ds(i * rows, rows), :] = value.astype(out.dtype)
    if ride:
        vector_ref, total_ref = refs[0], refs[3]
        came = take_vector(got_ref, blocks * rows, vector_ref.shape[1])
        total_ref[...] = settled_rows(vector_ref[...]) + came
        put_vector(total_ref[...], away_ref, blocks // 2 * rows)


def finish_kernel(*refs):
    vector_ref, refs = refs[0], refs[1:]
    down_ref, up_ref, out_ref, qkv_ref = refs[8:12]
    head_ref, bias_up_ref, bias_ref, gain_ref, shift_ref = refs[12:]
    rows, cols = out_ref.shape
    down, up, oq, kv = (
        refs[2 * i][...].astype(F32) + refs[2 * i + 1][:rows, :].astype(F32) for i in range(4)
    )
    down_ref[...] = down
    up_ref[...] = up
    out_ref[...] = oq[:, :cols]
    qkv_ref[0] = oq[:, cols:]
    qkv_ref[1] = kv[:, :cols]
    qkv_ref[2] = kv[:, cols:]
    total = vector_ref[...]
    if refs[5].shape[0] > rows:
        total = settled_rows(total) + take_vector(refs[5], rows, total.shape[1])
    bias_ref[...] = total[0:2]
    gain_ref[...] = total[2:4]
    shift_ref[...] = total[4:6]
    bias_up_ref[...] = total[6:7]
    head_ref[0:1, :] = total[7:8, :cols]
    head_ref[1:2, :] = total[7:8, cols : 2 * cols]


def levels(n):
    return [1 << i for i in reversed(range(n.bit_length() - 1))]


def build(nw, nc, nt):
    if nw != 2 or nt % 2 or nc & (nc - 1) or nt & (nt - 1):
        raise ValueError("mesh")
    sizes = {"weight": nw, "ctx": nc, "tensor": nt}

    def send(a, axis, bit=1):
        return lax.ppermute(a, axis, [(i, i ^ bit) for i in range(sizes[axis])])

    def settle(keep, sent):
        total = keep + send(sent, "tensor").astype(F32)
        bit = 2
        while bit < nt:
            sent = total.astype(BF)
            got = send(sent, "tensor", bit)
            total = sent.astype(F32) + got.astype(F32)
            bit *= 2
        return sent, got

    def gather(a):
        held, bit = [a], nc // 2
        while bit:
            held = held + [send(h, "ctx", bit) for h in held]
            bit //= 2
        return held

    def gather_few(a):
        held, bit = [a], nc // 2
        while bit:
            whole = held[0] if len(held) == 1 else jnp.concatenate(held, axis=0)
            held = held + [send(whole, "ctx", bit)]
            bit //= 2
        return held

    def owned(products, after, mines, ride=None):
        rows = products[0][0][3] // nc
        cols = sum(p[0][2][2] for p in products)
        blocks, extra, vector = nc // 2, 0, None
        if rows % 128 == 0:
            flat, terms, flops = [], [], 0
            for group in products:
                terms.append([])
                for stack, low, (b, first, wide), high in group:
                    pieces = [(len(flat) + i, count) for i, (_, count) in enumerate(stack)]
                    flat += [ref for ref, _ in stack] + [b]
                    terms[-1].append((pieces, low, (len(flat) - 1, first, wide)))
                    flops += 2 * b.shape[0] * high * wide
            spec, outs = None, ()
            if ride:
                tokens, *carried = ride
                spec = (tokens, *range(len(flat), len(flat) + 4))
                flat += carried
                extra = 24 * carried[0].shape[1] // cols
                outs = (arr(*carried[0].shape, F32),)
            away, stay, *rest = call(
                lambda *r: weight_kernel(nc, terms, rows, spec, *r),
                (arr(blocks * rows + extra, cols, BF), arr(blocks * rows, cols, BF)) + outs,
                mines[0],
                *flat,
                flops=flops,
                scalars=1,
            )
            vector = rest[0] if ride else None
        else:
            grad = []
            for group in products:
                value = 0.0
                for stack, low, (b, first, wide), high in group:
                    lhs = jnp.concatenate([r[:c, low : low + high] for r, c in stack], axis=0)
                    value = value + dot(lhs, b[: lhs.shape[0], first : first + wide], TN)
                grad.append(value.astype(BF))
            view = jnp.concatenate(grad, axis=1).reshape(blocks, 2, rows, cols)
            upper = mines[0][0] == 1
            away = jnp.where(upper, view[:, 0], view[:, 1]).reshape(blocks * rows, cols)
            stay = jnp.where(upper, view[:, 1], view[:, 0]).reshape(blocks * rows, cols)
        bit, level = 1, 1
        while True:
            got = send(away, "ctx", bit)
            got, stay, _ = lax.optimization_barrier((got, stay, after[0]))
            after = after[1:]
            bit *= 2
            if bit == nc:
                return stay, got, vector
            carried = (vector,) if extra else ()
            away, stay, *rest = call(
                lambda *r, blocks=blocks: middle_kernel(blocks, rows, *r),
                (arr(blocks // 2 * rows + extra, cols, BF), arr(blocks // 2 * rows, cols, F32))
                + tuple(arr(*v.shape, F32) for v in carried),
                mines[level], stay, got, *carried,
                scalars=1,
            )
            vector = rest[0] if extra else vector
            blocks, level = blocks // 2, level + 1

    def local(
        inputs, w_qkv, w_out, w_up, w_down, head_bias, up_bias, out_biases,
        norm_gains, norm_shifts, cotangent,
    ):
        tokens, width = inputs.shape[1], inputs.shape[2]
        half_t, half_d = tokens // 2, width // 2
        cols, hidden = w_qkv.shape[2], w_up.shape[1]
        rank = lax.axis_index("ctx")
        piece_at = rank * (half_d // nc)
        far_weight = lax.axis_index("weight") == 1
        far_core = jnp.bitwise_and(lax.axis_index("tensor"), 1) == 1
        ranks = rank.reshape(1)
        mines = [jnp.bitwise_and(ranks // bit, 1) for bit in reversed(levels(nc))]
        flags = far_weight.astype(jnp.int32).reshape(1)
        early = (piece_at, far_weight, far_core, ranks, flags, mines)
        (inputs, w_qkv, w_out, w_up, w_down, cotangent), early = lax.optimization_barrier(
            ((inputs, w_qkv, w_out, w_up, w_down, cotangent), early)
        )
        piece_at, far_weight, far_core, ranks, flags, mines = early

        def turn_d(a):
            return jnp.where(far_weight, jnp.concatenate([a[:, half_d:], a[:, :half_d]], 1), a)

        def turn_t(a):
            return jnp.where(far_core, jnp.concatenate([a[half_t:], a[:half_t]], 0), a)

        wk = w_qkv[:, 1]
        wk_far = send(wk, "weight")
        piece = lax.dynamic_slice_in_dim(w_down, piece_at, half_d // nc, 0)
        piece = send(piece, "weight")
        up_far = send(w_up, "weight")
        pieces = gather(piece)

        x = turn_t(turn_d(inputs[0]))
        x_own = x[:half_t]
        w_qkv, x = lax.optimization_barrier((w_qkv, x))
        wq, wv = w_qkv[:, 0], w_qkv[:, 2]
        wv_far = send(wv, "weight")
        wqo = jnp.concatenate([wq, w_out], axis=1)
        wqo_far = send(wqo, "weight")
        cot = turn_t(turn_d(cotangent[0]))[:half_t]
        out_b, gains, shifts = turn_d(out_biases), turn_d(norm_gains), turn_d(norm_shifts)
        x_lo, x_hi = x[:, :half_d], x[:, half_d:]

        k = (dot(x_lo, wk, NN) + dot(x_hi, wk_far, NN)).astype(BF)
        ks = gather(k)
        v = (dot(x_lo, wv, NN) + dot(x_hi, wv_far, NN) + head_bias[1]).astype(BF)
        vs = gather(v)
        q = dot(x_lo, wq, NN) + dot(x_hi, wqo_far[:, :cols], NN) + head_bias[0]
        q = q.astype(BF) * BF(HD**-0.5)
        qs = gather_few(q)

        part = (arr(half_t, width, F32), arr(half_t, width, BF))
        attended, lse, keep, sent = attend(q, wqo, wqo_far, ks, vs)
        sent, got = settle(keep, sent)
        mixed_one, normed_one, inverse_one, mixed_own = call(
            norm_one_kernel,
            (part[0], part[0], arr(half_t, 128, F32), part[1]),
            sent, got, x_own, out_b, gains, shifts,
        )
        mixed_got = send(mixed_own, "tensor")
        big = 2 * tokens * width * hidden
        pre_act, act, mixed_hi = call(
            up_kernel,
            (arr(tokens, hidden, F32), arr(tokens, hidden, BF), arr(tokens, half_d, BF)),
            mixed_own, mixed_got, w_up, up_far, up_bias.reshape(1, hidden),
            flops=big,
        )
        mixed_mate = send(mixed_hi, "weight")
        down_far, keep, sent = call(
            down_kernel,
            (arr(half_d, hidden, BF),) + part,
            ranks, act, w_down, *pieces,
            flops=big, scalars=1,
        )
        sent, got = settle(keep, sent)
        act_mate = send(act, "weight")
        pair, grad_two, sums_two = call(
            norm_two_kernel,
            (arr(tokens, width, BF), part[0], arr(3, width, F32)),
            sent, got, mixed_one, cot, out_b, gains, shifts,
        )
        pair_got = send(pair, "tensor")
        two_hi = jnp.concatenate([pair[:half_t, half_d:], pair_got[:half_t, half_d:]], axis=0)
        two_mate = send(two_hi, "weight")
        grad_pre, grad_up_b, keep, sent = call(
            back_kernel,
            (arr(tokens, hidden, BF), arr(1, hidden, F32)) + part,
            pair, pair_got, w_down, down_far, pre_act, w_up, up_far,
            flops=2 * big,
        )
        sent, got = settle(keep, sent)
        pre_mate = send(grad_pre, "weight")
        one_own, grad_one = call(
            norm_back_kernel,
            (arr(half_t + 32, width, BF), part[0]),
            sent, got, grad_two, normed_one, inverse_one, gains, sums_two,
        )
        one_got = send(one_own, "tensor")
        msg, bundle_own, vector = pack_message(
            flags, one_own, one_got, wqo, wqo_far, attended, lse, x, grad_up_b
        )
        msgs = gather(msg)
        bundle = send(bundle_own, "weight")
        dq = query_grads(q, msg, attended, lse, ks, vs)
        dq_mate = send(dq, "weight")
        dkv = key_grads(k, v, qs, msgs)

        dkv_mate = send(dkv, "weight")
        keep, sent = call(
            input_kernel, part, dq, dkv, wqo, wk, wv, wqo_far, wk_far, wv_far,
            flops=6 * tokens * width * cols,
        )
        late = [sent] * 8

        def term(stack, b, low=0, first=0, wide=None):
            return ([(r, r.shape[0] if c is None else c) for r, c in stack], low,
                    (b, first, b.shape[1] if wide is None else wide), half_d)

        grad_w_down = owned(
            [[term([(pair, half_t), (pair_got, half_t)], act), term([(two_mate, None)], act_mate)]],
            [dq] + late,
            mines,
        )
        grad_w_up = owned(
            [[
                term([(mixed_own, None), (mixed_got, None)], grad_pre),
                term([(mixed_mate, None)], pre_mate),
            ]],
            late,
            mines,
        )
        oq_grad = owned(
            [
                [
                    term([(one_own, half_t), (one_got, half_t)], attended),
                    term([(bundle, tokens)], bundle, first=width, wide=cols),
                ],
                [term([(x, None)], dq), term([(bundle, tokens)], dq_mate, low=half_d)],
            ],
            late,
            mines,
            (tokens, vector, bundle, dq, dq_mate),
        )
        sent, got = settle(keep, sent)
        grad_wkv = owned(
            [[term([(x, None)], dkv), term([(bundle, tokens)], dkv_mate, low=half_d)]], late, mines
        )
        grad_own = (grad_one + (sent.astype(F32) + got.astype(F32))).astype(BF)
        grad_got = send(grad_own, "tensor")
        grad_input = turn_d(turn_t(jnp.concatenate([grad_own, grad_got], axis=0)))
        pair, pair_got, _ = lax.optimization_barrier((pair, pair_got, late[0]))
        layer_out = turn_d(turn_t(jnp.concatenate([pair[half_t:], pair_got[half_t:]], axis=0)))

        if half_d // nc % 128:
            rows = join_rows(bundle[tokens:, :width], 8) + vector
            sums = join_rows(dq[tokens:], 1) + join_rows(dq_mate[tokens:], 1)
            vector = jnp.concatenate(
                [rows[:7], jnp.concatenate([sums, rows[7:, cols:]], axis=1)], axis=0
            )
            bit = 1
            while bit < nc:
                vector = vector + send(vector, "ctx", bit)
                bit *= 2
        else:
            vector = oq_grad[2]
        terms = [a_ for triple in (grad_w_down, grad_w_up, oq_grad, grad_wkv) for a_ in triple[:2]]
        terms, layer_out, grad_input = lax.optimization_barrier((terms, layer_out, grad_input))
        block = half_d // nc
        down_grad, up_grad, out_grad, qkv_grad, head, up_row, bias, gain, shift = call(
            finish_kernel,
            (arr(block, hidden, F32), arr(block, hidden, F32), arr(block, cols, F32),
             jax.ShapeDtypeStruct((3, block, cols), F32), arr(2, cols, F32), arr(1, hidden, F32))
            + (arr(2, width, F32),) * 3,
            vector, *terms,
        )
        return (
            layer_out[None],
            grad_input[None],
            jnp.transpose(qkv_grad, (1, 0, 2)),
            out_grad,
            up_grad,
            down_grad,
            head,
            up_row[0],
            bias,
            gain,
            shift,
        )

    return local


def solution(mesh):
    return jax.shard_map(
        build(mesh.shape["weight"], mesh.shape["ctx"], mesh.shape["tensor"]),
        mesh=mesh,
        in_specs=(
            P("weight", "ctx", None),
            P("weight", None, "tensor"),
            P("weight", "tensor"),
            P("weight", "tensor"),
            P("weight", "tensor"),
            P(None, "tensor"),
            P("tensor"),
            P(),
            P(),
            P(),
            P("weight", "ctx", None),
        ),
        out_specs=(
            P("weight", "ctx", None),
            P("weight", "ctx", None),
            P(("weight", "ctx"), None, "tensor"),
            P(("weight", "ctx"), "tensor"),
            P(("weight", "ctx"), "tensor"),
            P(("weight", "ctx"), "tensor"),
            P(None, "tensor"),
            P("tensor"),
            P(),
            P(),
            P(),
        ),
        check_vma=False,
    )
```

```python
import math

import jax
import jax.numpy as jnp
from jax import lax
from jax.experimental import pallas as pl
from jax.experimental.pallas import tpu as pltpu
from jax.sharding import PartitionSpec as P


HD = 64
ROOM = pltpu.CompilerParams(vmem_limit_bytes=20 << 20)
BF = jnp.bfloat16
F32 = jnp.float32


norm_epsilon = 1e-05
inv_root_two = 1.0 / math.sqrt(2.0)
inv_root_tau = 1.0 / math.sqrt(2.0 * math.pi)

NT = (((1,), (1,)), ((), ()))
NN = (((1,), (0,)), ((), ()))
TN = (((0,), (0,)), ((), ()))


def dot(a, b, dims):
    return lax.dot_general(a, b, dims, preferred_element_type=F32)


def layer_stats(hidden):
    mean_row = jnp.mean(hidden, axis=-1, keepdims=True)
    centred = hidden - mean_row
    inverse_spread = lax.rsqrt(jnp.mean(centred * centred, axis=-1, keepdims=True) + norm_epsilon)
    return (centred * inverse_spread, inverse_spread)


def layer_back(grad_norm, normed, inverse_spread):
    return inverse_spread * (
        grad_norm
        - jnp.mean(grad_norm, axis=-1, keepdims=True)
        - normed * jnp.mean(grad_norm * normed, axis=-1, keepdims=True)
    )


def gelu_value(pre_act):
    return 0.5 * pre_act * (1.0 + lax.erf(pre_act * inv_root_two))


def gelu_slope(pre_act):
    return (
        0.5 * (1.0 + lax.erf(pre_act * inv_root_two))
        + pre_act * jnp.exp(-0.5 * pre_act * pre_act) * inv_root_tau
    )


def head_mask(shape, head):
    lane = lax.broadcasted_iota(jnp.int32, shape, 1)
    return (lane >= head * HD) & (lane < (head + 1) * HD)


def as_rows(columns, rows):
    tokens = columns[0].shape[0]
    lane = lax.broadcasted_iota(jnp.int32, (tokens, 128), 1)
    tile = jnp.zeros((tokens, 128), F32)
    for i, col in enumerate(columns):
        tile = jnp.where(lane == i, col, tile)
    return tile.T[:rows]


def attend_kernel(n, heads, *refs):
    q_ref, near_ref, far_ref = refs[:3]
    k_refs, v_refs = refs[3 : 3 + n], refs[3 + n : 3 + 2 * n]
    out_ref, lse_ref, keep_ref, sent_ref = refs[3 + 2 * n :]
    q = q_ref[...]
    out = jnp.zeros(q.shape, F32)
    lses = []
    for h in range(heads):
        mask = head_mask(q.shape, h)
        qh = jnp.where(mask, q, jnp.zeros_like(q))
        scores = [dot(qh, k[...], NT) for k in k_refs]
        top = scores[0]
        for s in scores[1:]:
            top = jnp.maximum(top, s)
        top = jnp.max(top, axis=1, keepdims=True)
        total = jnp.zeros(top.shape, F32)
        acc = jnp.zeros(q.shape, F32)
        psum = None
        for s, v in zip(scores, v_refs):
            p = jnp.exp(s - top)
            psum = p if psum is None else psum + p
            acc = acc + dot(p.astype(BF), v[...], NN)
        total = jnp.sum(psum, axis=1, keepdims=True)
        out = jnp.where(mask, acc / total, out)
        lses.append(top + jnp.log(total))
    out_ref[...] = out.astype(BF)
    lse_ref[...] = as_rows(lses, heads)
    weight = pl.ds(near_ref.shape[1] - q.shape[1], q.shape[1])
    out_kernel(out_ref, near_ref.at[:, weight], far_ref.at[:, weight], keep_ref, sent_ref)


def attend(q, near, far, ks, vs):
    n, (tokens, cols) = len(ks), q.shape
    width = 2 * near.shape[0]
    heads = cols // HD
    keys = n * tokens
    return pl.pallas_call(
        lambda *r: attend_kernel(n, heads, *r),
        out_shape=(
            jax.ShapeDtypeStruct((tokens, cols), BF),
            jax.ShapeDtypeStruct((heads, tokens), F32),
            jax.ShapeDtypeStruct((tokens // 2, width), F32),
            jax.ShapeDtypeStruct((tokens // 2, width), BF),
        ),
        cost_estimate=pl.CostEstimate(
            flops=4 * tokens * keys * cols * heads,
            bytes_accessed=2 * (2 * keys + 2 * tokens) * cols,
            transcendentals=tokens * keys * heads,
        ),
        name="attend",
        compiler_params=ROOM,
    )(q, near, far, *ks, *vs)


def split_rows(rows):
    high = rows.astype(BF)
    rest = rows - high.astype(F32)
    middle = rest.astype(BF)
    low = (rest - middle.astype(F32)).astype(BF)
    return [high, middle, low]


def join_rows(parts, count):
    wide = parts.astype(F32)
    return wide[:count] + wide[count : 2 * count] + wide[2 * count : 3 * count]


def stack_rows(parts, rows):
    parts = [p.astype(F32) for p in parts]
    spare = rows - sum(p.shape[0] for p in parts)
    if spare:
        parts.append(jnp.zeros((spare, parts[0].shape[1]), F32))
    return jnp.concatenate(parts, axis=0).astype(BF)


def folded(rows, cols):
    return jnp.concatenate([rows[:, i : i + cols] for i in range(0, rows.shape[1], cols)], axis=0)


def unfolded(rows, count):
    return jnp.concatenate(
        [rows[i : i + count] for i in range(0, rows.shape[0], count)], axis=1
    )


def settled_rows(rows):
    high, middle, low = split_rows(rows)
    return high.astype(F32) + middle.astype(F32) + low.astype(F32)


def message_rows(tokens, heads):
    return tokens + -(-6 * heads // 16) * 16


def pack_kernel(
    heads, flag_ref, own_ref, got_ref, near_ref, far_ref, at_ref, lse_ref, x_ref, up_ref, *outs
):
    msg_ref, bundle_ref, vector_ref = outs
    half = near_ref.shape[0]
    tokens, cols = at_ref.shape
    part = tokens // 2
    one = jnp.concatenate([own_ref[:part, :], got_ref[:part, :]], axis=0)
    bundle_ref[:part, :half] = own_ref[:part, half:]
    bundle_ref[:part, pl.ds(half, half)] = x_ref[:part, pl.ds(half, half)]
    bundle_ref[:part, pl.ds(2 * half, cols)] = at_ref[:part, :]
    bundle_ref[:part, pl.ds(2 * half + cols, cols)] = at_ref[part:, :]
    out = pl.ds(near_ref.shape[1] - cols, cols)
    da = dot(one[:, :half], near_ref[:, out], NN) + dot(one[:, half:], far_ref[:, out], NN)
    da = da.astype(BF)
    rows = join_rows(own_ref[part:, :], 6) + join_rows(got_ref[part:, :], 6)
    turned = jnp.concatenate([rows[:, half:], rows[:, :half]], axis=1)
    vector_ref[0:6, :] = jnp.where(flag_ref[0] == 1, turned, rows)
    vector_ref[6:7, :] = up_ref[...]
    vector_ref[7:8, :] = jnp.zeros((1, 2 * half), F32)
    vector_ref[7:8, pl.ds(cols, cols)] = jnp.sum(da.astype(F32), axis=0, keepdims=True)
    extra = bundle_ref.shape[0] - part
    bundle_ref[part:, : 2 * half] = stack_rows(split_rows(vector_ref[...]), extra)
    bundle_ref[part:, pl.ds(2 * half, 2 * cols)] = jnp.zeros((extra, 2 * cols), BF)
    prod = da.astype(F32) * at_ref[...].astype(F32)
    deltas = []
    for h in range(heads):
        mask = head_mask(da.shape, h)
        deltas.append(jnp.sum(jnp.where(mask, prod, 0.0), axis=1, keepdims=True))
    rows = split_rows(lse_ref[...]) + split_rows(as_rows(deltas, heads))
    msg_ref[:tokens, :] = da
    msg_ref[tokens:, :] = stack_rows(rows, msg_ref.shape[0] - tokens)


def pack_message(flags, own, got, near, far, attended, lse, x, up_row):
    tokens, cols = attended.shape
    width, heads = own.shape[1], cols // HD
    if tokens != cols or up_row.shape[1] != width or 2 * cols > width:
        raise ValueError("message shape")
    return call(
        lambda *r: pack_kernel(heads, *r),
        (
            arr(message_rows(tokens, heads), cols, BF),
            arr(tokens // 2 + 32, width + 2 * cols, BF),
            arr(8, width, F32),
        ),
        flags, own, got, near, far, attended, lse, x, up_row,
        flops=2 * tokens * width * cols, scalars=1,
    )


def query_kernel(n, heads, *refs):
    q_ref, da_ref, at_ref, lse_ref = refs[:4]
    k_refs, v_refs = refs[4 : 4 + n], refs[4 + n : 4 + 2 * n]
    dq_ref = refs[4 + 2 * n]
    q = q_ref[...]
    tokens = q.shape[0]
    da = da_ref[:tokens, :]
    prod = da.astype(F32) * at_ref[...].astype(F32)
    lse_pad = jnp.concatenate([lse_ref[...], jnp.zeros((128 - heads, tokens), F32)], axis=0).T
    out = jnp.zeros(q.shape, F32)
    for h in range(heads):
        mask = head_mask(q.shape, h)
        zero = jnp.zeros_like(q)
        qh, dah = jnp.where(mask, q, zero), jnp.where(mask, da, zero)
        delta = jnp.sum(jnp.where(mask, prod, 0.0), axis=1, keepdims=True)
        lse = lse_pad[:, h : h + 1]
        acc = jnp.zeros(q.shape, F32)
        for k, v in zip(k_refs, v_refs):
            p = jnp.exp(dot(qh, k[...], NT) - lse)
            ds = (p * (dot(dah, v[...], NT) - delta)).astype(BF)
            acc = acc + dot(ds, k[...], NN)
        out = jnp.where(mask, acc, out)
    out = out * (HD**-0.5)
    dq_ref[:tokens, :] = out.astype(BF)
    sums = jnp.sum(out, axis=0, keepdims=True)
    dq_ref[tokens:, :] = stack_rows(split_rows(sums), dq_ref.shape[0] - tokens)


def query_grads(q, msg, attended, lse, ks, vs):
    n, (tokens, cols) = len(ks), q.shape
    heads, keys = cols // HD, len(ks) * q.shape[0]
    return pl.pallas_call(
        lambda *r: query_kernel(n, heads, *r),
        out_shape=jax.ShapeDtypeStruct((tokens + 16, cols), BF),
        cost_estimate=pl.CostEstimate(
            flops=6 * tokens * keys * cols * heads,
            bytes_accessed=2 * (2 * keys + 4 * tokens) * cols,
            transcendentals=tokens * keys * heads,
        ),
        name="query_grads",
        compiler_params=ROOM,
    )(q, msg, attended, lse, *ks, *vs)


def key_kernel(m, n, heads, *refs):
    k_ref, v_ref = refs[:2]
    tokens, cols = k_ref.shape
    qs = [
        r.at[pl.ds(i * tokens, tokens)]
        for r in refs[2 : 2 + m]
        for i in range(r.shape[0] // tokens)
    ]
    msgs = refs[2 + m : 2 + m + n]
    out_ref = refs[2 + m + n]
    k, v = k_ref[...], v_ref[...]
    stats = []
    for msg in msgs:
        rows = msg[tokens:, :].astype(F32)
        part = [rows[i * heads : (i + 1) * heads] for i in range(6)]
        stats.append((part[0] + part[1] + part[2], part[3] + part[4] + part[5]))
    dk, dv = jnp.zeros(k.shape, F32), jnp.zeros(k.shape, F32)
    for h in range(heads):
        mask = head_mask(k.shape, h)
        zero = jnp.zeros_like(k)
        kh, vh = jnp.where(mask, k, zero), jnp.where(mask, v, zero)
        dk_acc, dv_acc = jnp.zeros(k.shape, F32), jnp.zeros(k.shape, F32)
        for q, msg, (lse, delta) in zip(qs, msgs, stats):
            da = msg[:tokens, :]
            p = jnp.exp(dot(kh, q[...], NT) - lse[h : h + 1, :])
            dv_acc = dv_acc + dot(p.astype(BF), da, NN)
            ds = (p * (dot(vh, da, NT) - delta[h : h + 1, :])).astype(BF)
            dk_acc = dk_acc + dot(ds, q[...], NN)
        dk, dv = jnp.where(mask, dk_acc, dk), jnp.where(mask, dv_acc, dv)
    out_ref[:, :cols] = dk.astype(BF)
    out_ref[:, cols:] = dv.astype(BF)


def key_grads(k, v, qs, msgs):
    m, n, (tokens, cols) = len(qs), len(msgs), k.shape
    heads, rows = cols // HD, n * tokens
    return pl.pallas_call(
        lambda *r: key_kernel(m, n, heads, *r),
        out_shape=jax.ShapeDtypeStruct((tokens, 2 * cols), BF),
        cost_estimate=pl.CostEstimate(
            flops=8 * tokens * rows * cols * heads,
            bytes_accessed=2 * (2 * rows + 4 * tokens) * cols,
            transcendentals=tokens * rows * heads,
        ),
        name="key_grads",
        compiler_params=ROOM,
    )(k, v, *qs, *msgs)


def arr(rows, cols, dtype):
    return jax.ShapeDtypeStruct((rows, cols), dtype)


def call(kernel, outs, *args, flops=0, scalars=0):
    outs_list = outs if isinstance(outs, (tuple, list)) else (outs,)
    total = sum(math.prod(a.shape) * a.dtype.itemsize for a in list(args) + list(outs_list))
    return pl.pallas_call(
        kernel,
        out_shape=outs,
        in_specs=[
            pl.BlockSpec(memory_space=pltpu.SMEM if i < scalars else pltpu.VMEM)
            for i in range(len(args))
        ],
        cost_estimate=pl.CostEstimate(flops=flops, bytes_accessed=total, transcendentals=0),
        compiler_params=ROOM,
    )(*args)


def column_blocks(cols):
    size = 256 if cols % 256 == 0 else cols
    return [pl.ds(i, size) for i in range(0, cols, size)]


def put_partial(block, value, keep_ref, sent_ref):
    half = keep_ref.shape[0]
    keep_ref[:, block] = value[:half]
    sent_ref[:, block] = value[half:].astype(BF)


def out_kernel(at_ref, near_ref, far_ref, keep_ref, sent_ref):
    at = at_ref[...]
    half = near_ref.shape[0]
    for start, ref in ((0, near_ref), (half, far_ref)):
        for rows in column_blocks(half):
            value = dot(at, ref[rows, :], NT)
            put_partial(pl.ds(start + rows.start, rows.size), value, keep_ref, sent_ref)


def norm_one_kernel(sent_ref, got_ref, x_ref, bias_ref, gain_ref, shift_ref, *outs):
    mixed_ref, normed_ref, inverse_ref, own_ref = outs
    summed = sent_ref[...].astype(F32) + got_ref[...].astype(F32)
    hidden = x_ref[...].astype(F32) + summed + bias_ref[0:1, :]
    normed, inverse = layer_stats(hidden)
    mixed = normed * gain_ref[0:1, :] + shift_ref[0:1, :]
    mixed_ref[...] = mixed
    normed_ref[...] = normed
    inverse_ref[...] = jnp.broadcast_to(inverse, inverse_ref.shape)
    own_ref[...] = mixed.astype(BF)


def up_kernel(own_ref, got_ref, near_ref, far_ref, bias_ref, pre_ref, act_ref, high_ref):
    half = near_ref.shape[0]
    mixed = jnp.concatenate([own_ref[...], got_ref[...]], axis=0)
    low, high = mixed[:, :half], mixed[:, half:]
    high_ref[...] = high
    for block in column_blocks(near_ref.shape[1]):
        pre = dot(low, near_ref[:, block], NN) + dot(high, far_ref[:, block], NN)
        pre = pre + bias_ref[:, block]
        pre_ref[:, block] = pre
        act_ref[:, block] = gelu_value(pre).astype(BF)


def offsets(n):
    held = [0]
    for bit in levels(n):
        held = held + [i ^ bit for i in held]
    return held


def down_kernel(rank_ref, act_ref, near_ref, *refs):
    pieces, (far_ref, keep_ref, sent_ref) = refs[:-3], refs[-3:]
    rows = pieces[0].shape[0]
    for offset, piece in zip(offsets(len(pieces)), pieces):
        at = pl.multiple_of(jnp.bitwise_xor(rank_ref[0], offset) * rows, rows)
        far_ref[pl.ds(at, rows), :] = piece[...]
    out_kernel(act_ref, near_ref, far_ref, keep_ref, sent_ref)


def norm_two_kernel(
    sent_ref, got_ref, mixed_ref, cot_ref, bias_ref, gain_ref, shift_ref, pair_ref, grad_ref, sum_ref
):
    summed = sent_ref[...].astype(F32) + got_ref[...].astype(F32)
    normed, inverse = layer_stats(mixed_ref[...] + summed + bias_ref[1:2, :])
    gain = gain_ref[1:2, :]
    cot = cot_ref[...].astype(F32)
    grad = layer_back(cot * gain, normed, inverse)
    half = grad.shape[0]
    pair_ref[:half, :] = grad.astype(BF)
    pair_ref[half:, :] = (normed * gain + shift_ref[1:2, :]).astype(BF)
    grad_ref[...] = grad
    sum_ref[0:1, :] = jnp.sum(grad, axis=0, keepdims=True)
    sum_ref[1:2, :] = jnp.sum(cot * normed, axis=0, keepdims=True)
    sum_ref[2:3, :] = jnp.sum(cot, axis=0, keepdims=True)


def back_kernel(own_ref, got_ref, dn_ref, df_ref, pre_ref, un_ref, uf_ref, *outs):
    grad_ref, sum_ref, keep_ref, sent_ref = outs
    half = dn_ref.shape[0]
    tokens = own_ref.shape[0] // 2
    two = jnp.concatenate([own_ref[:tokens, :], got_ref[:tokens, :]], axis=0)
    low, high = two[:, :half], two[:, half:]
    for block in column_blocks(dn_ref.shape[1]):
        grad = dot(low, dn_ref[:, block], NN) + dot(high, df_ref[:, block], NN)
        grad = grad * gelu_slope(pre_ref[:, block])
        sum_ref[:, block] = jnp.sum(grad, axis=0, keepdims=True)
        grad_ref[:, block] = grad.astype(BF)
    out_kernel(grad_ref, un_ref, uf_ref, keep_ref, sent_ref)


def norm_back_kernel(
    sent_ref, got_ref, two_ref, normed_ref, inverse_ref, gain_ref, sums_ref, *outs
):
    own_ref, grad_ref = outs
    normed = normed_ref[...]
    mixed = two_ref[...] + (sent_ref[...].astype(F32) + got_ref[...].astype(F32))
    grad = layer_back(mixed * gain_ref[0:1, :], normed, inverse_ref[:, 0:1])
    tokens = grad.shape[0]
    own_ref[:tokens, :] = grad.astype(BF)
    grad_ref[...] = grad
    sums = []
    for i, value in enumerate((grad, mixed * normed, mixed)):
        sums += [jnp.sum(value, axis=0, keepdims=True), sums_ref[i : i + 1, :]]
    rows = own_ref.shape[0] - tokens
    own_ref[tokens:, :] = stack_rows(split_rows(jnp.concatenate(sums, axis=0)), rows)


def input_kernel(dq_ref, dkv_ref, *refs):
    near, far, (keep_ref, sent_ref) = refs[:3], refs[3:6], refs[6:]
    dq = dq_ref[: dkv_ref.shape[0], :]
    cols, half = dq.shape[1], near[0].shape[0]
    dk, dv = dkv_ref[:, :cols], dkv_ref[:, cols:]
    for start, (q_ref, k_ref, v_ref) in ((0, near), (half, far)):
        for rows in column_blocks(half):
            value = dot(dq, q_ref[rows, pl.ds(0, cols)], NT)
            value = value + dot(dk, k_ref[rows, :], NT) + dot(dv, v_ref[rows, :], NT)
            put_partial(pl.ds(start + rows.start, rows.size), value, keep_ref, sent_ref)


def weight_kernel(n, terms, rows, ride, mine_ref, *refs):
    count = 3 if ride else 2
    ins, outs = refs[:-count], refs[-count:]
    away_ref, stay_ref = outs[:2]
    mine = mine_ref[0]
    for i in range(n // 2):
        for out, side in ((away_ref, 1 - mine), (stay_ref, mine)):
            at = (2 * i + side) * rows
            col = 0
            for group in terms:
                value = None
                for pieces, low, b in group:
                    block = pl.ds(pl.multiple_of(at + low, 128), rows)
                    a = [ins[k][pl.ds(0, tall), block] for k, tall in pieces]
                    a = a[0] if len(a) == 1 else jnp.concatenate(a, axis=0)
                    b = [ins[k][pl.ds(0, tall), pl.ds(first, cols)] for k, tall, first, cols in b]
                    b = b[0] if len(b) == 1 else jnp.concatenate(b, axis=0)
                    term = dot(a, b, TN)
                    value = term if value is None else value + term
                out[pl.ds(i * rows, rows), pl.ds(col, value.shape[1])] = value.astype(BF)
                col += value.shape[1]
    if ride:
        part, tokens, vector, bundle, dq, dq_mate = ride
        width = ins[vector].shape[1]
        rows_x = settled_rows(ins[vector][...])
        outs[2][...] = rows_x + join_rows(ins[bundle][part:, :width], 8)
        sums = join_rows(ins[dq][tokens:, :], 1) + join_rows(ins[dq_mate][tokens:, :], 1)
        outs[2][7:8, pl.ds(0, sums.shape[1])] = sums
        put_vector(outs[2][...], away_ref, n // 2 * rows)


def put_vector(vector, away_ref, first):
    cols = away_ref.shape[1]
    parts = [folded(p.astype(F32), cols).astype(BF) for p in split_rows(vector)]
    away_ref[first:, :] = stack_rows(parts, away_ref.shape[0] - first)


def take_vector(got_ref, first, width):
    cols = got_ref.shape[1]
    return unfolded(join_rows(got_ref[first:, :], 8 * width // cols), 8)


def middle_kernel(blocks, rows, mine_ref, stay_ref, got_ref, *refs):
    mine = mine_ref[0]
    ride = len(refs) == 4
    away_ref, kept_ref = refs[1:3] if ride else refs
    for i in range(blocks // 2):
        for out, side in ((away_ref, 1 - mine), (kept_ref, mine)):
            at = pl.ds(pl.multiple_of((2 * i + side) * rows, rows), rows)
            value = stay_ref[at, :].astype(F32) + got_ref[at, :].astype(F32)
            out[pl.ds(i * rows, rows), :] = value.astype(out.dtype)
    if ride:
        vector_ref, total_ref = refs[0], refs[3]
        came = take_vector(got_ref, blocks * rows, vector_ref.shape[1])
        total_ref[...] = settled_rows(vector_ref[...]) + came
        put_vector(total_ref[...], away_ref, blocks // 2 * rows)


def add_kernel(down_ref, down_got_ref, up_ref, up_got_ref, down_out_ref, up_out_ref):
    down_out_ref[...] = down_ref[...].astype(F32) + down_got_ref[...].astype(F32)
    up_out_ref[...] = up_ref[...].astype(F32) + up_got_ref[...].astype(F32)


def finish_kernel(*refs):
    vector_ref, refs = refs[0], refs[1:]
    out_ref, qkv_ref = refs[4:6]
    head_ref, bias_up_ref, bias_ref, gain_ref, shift_ref = refs[6:]
    rows, cols = out_ref.shape
    oq, kv = (
        refs[2 * i][...].astype(F32) + refs[2 * i + 1][:rows, :].astype(F32) for i in range(2)
    )
    out_ref[...] = oq[:, :cols]
    qkv_ref[0] = oq[:, cols:]
    qkv_ref[1] = kv[:, :cols]
    qkv_ref[2] = kv[:, cols:]
    total = vector_ref[...]
    if refs[1].shape[0] > rows:
        total = settled_rows(total) + take_vector(refs[1], rows, total.shape[1])
    bias_ref[...] = total[0:2]
    gain_ref[...] = total[2:4]
    shift_ref[...] = total[4:6]
    bias_up_ref[...] = total[6:7]
    head_ref[0:1, :] = total[7:8, :cols]
    head_ref[1:2, :] = total[7:8, cols : 2 * cols]


def levels(n):
    return [1 << i for i in reversed(range(n.bit_length() - 1))]


def build(nw, nc, nt):
    if nw != 2 or nt % 2 or nc & (nc - 1) or nt & (nt - 1):
        raise ValueError("mesh")
    sizes = {"weight": nw, "ctx": nc, "tensor": nt}

    def send(a, axis, bit=1):
        return lax.ppermute(a, axis, [(i, i ^ bit) for i in range(sizes[axis])])

    def settle(keep, sent):
        total = keep + send(sent, "tensor").astype(F32)
        bit = 2
        while bit < nt:
            sent = total.astype(BF)
            got = send(sent, "tensor", bit)
            total = sent.astype(F32) + got.astype(F32)
            bit *= 2
        return sent, got

    def gather(a):
        held, bit = [a], nc // 2
        while bit:
            held = held + [send(h, "ctx", bit) for h in held]
            bit //= 2
        return held

    def gather_few(a):
        held, bit = [a], nc // 2
        while bit:
            whole = held[0] if len(held) == 1 else jnp.concatenate(held, axis=0)
            held = held + [send(whole, "ctx", bit)]
            bit //= 2
        return held

    def owned(products, after, mines, ride=None):
        rows = products[0][0][3] // nc
        cols = sum(p[0][2][0][3] for p in products)
        blocks, extra, vector = nc // 2, 0, None
        if rows % 128 == 0:
            flat, terms, flops = [], [], 0
            for group in products:
                terms.append([])
                for stack, low, b, high in group:
                    pieces = [(len(flat) + i, count) for i, (_, count) in enumerate(stack)]
                    flat += [ref for ref, _ in stack]
                    others = [(len(flat) + i, *piece[1:]) for i, piece in enumerate(b)]
                    flat += [piece[0] for piece in b]
                    terms[-1].append((pieces, low, others))
                    flops += sum(2 * tall * high * wide for _, tall, _, wide in b)
            spec, outs = None, ()
            if ride:
                part, tokens, *carried = ride
                spec = (part, tokens, *range(len(flat), len(flat) + 4))
                flat += carried
                extra = 24 * carried[0].shape[1] // cols
                outs = (arr(*carried[0].shape, F32),)
            away, stay, *rest = call(
                lambda *r: weight_kernel(nc, terms, rows, spec, *r),
                (arr(blocks * rows + extra, cols, BF), arr(blocks * rows, cols, BF)) + outs,
                mines[0],
                *flat,
                flops=flops,
                scalars=1,
            )
            vector = rest[0] if ride else None
        else:
            grad = []
            for group in products:
                value = 0.0
                for stack, low, b, high in group:
                    lhs = jnp.concatenate([r[:c, low : low + high] for r, c in stack], axis=0)
                    rhs = jnp.concatenate([r[:c, f : f + wide] for r, c, f, wide in b], axis=0)
                    value = value + dot(lhs, rhs, TN)
                grad.append(value.astype(BF))
            view = jnp.concatenate(grad, axis=1).reshape(blocks, 2, rows, cols)
            upper = mines[0][0] == 1
            away = jnp.where(upper, view[:, 0], view[:, 1]).reshape(blocks * rows, cols)
            stay = jnp.where(upper, view[:, 1], view[:, 0]).reshape(blocks * rows, cols)
        bit, level = 1, 1
        while True:
            got = send(away, "ctx", bit)
            got, stay, _ = lax.optimization_barrier((got, stay, after[0]))
            after = after[1:]
            bit *= 2
            if bit == nc:
                return stay, got, vector
            carried = (vector,) if extra else ()
            away, stay, *rest = call(
                lambda *r, blocks=blocks: middle_kernel(blocks, rows, *r),
                (arr(blocks // 2 * rows + extra, cols, BF), arr(blocks // 2 * rows, cols, F32))
                + tuple(arr(*v.shape, F32) for v in carried),
                mines[level], stay, got, *carried,
                scalars=1,
            )
            vector = rest[0] if extra else vector
            blocks, level = blocks // 2, level + 1

    def local(
        inputs, w_qkv, w_out, w_up, w_down, head_bias, up_bias, out_biases,
        norm_gains, norm_shifts, cotangent,
    ):
        tokens, width = inputs.shape[1], inputs.shape[2]
        half_t, half_d = tokens // 2, width // 2
        cols, hidden = w_qkv.shape[2], w_up.shape[1]
        rank = lax.axis_index("ctx")
        piece_at = rank * (half_d // nc)
        far_weight = lax.axis_index("weight") == 1
        far_core = jnp.bitwise_and(lax.axis_index("tensor"), 1) == 1
        ranks = rank.reshape(1)
        mines = [jnp.bitwise_and(ranks // bit, 1) for bit in reversed(levels(nc))]
        flags = far_weight.astype(jnp.int32).reshape(1)
        early = (piece_at, far_weight, far_core, ranks, flags, mines)
        (inputs, w_qkv, w_out, w_up, w_down, cotangent), early = lax.optimization_barrier(
            ((inputs, w_qkv, w_out, w_up, w_down, cotangent), early)
        )
        piece_at, far_weight, far_core, ranks, flags, mines = early

        def turn_d(a):
            return jnp.where(far_weight, jnp.concatenate([a[:, half_d:], a[:, :half_d]], 1), a)

        def turn_t(a):
            return jnp.where(far_core, jnp.concatenate([a[half_t:], a[:half_t]], 0), a)

        wk = w_qkv[:, 1]
        wk_far = send(wk, "weight")
        piece = lax.dynamic_slice_in_dim(w_down, piece_at, half_d // nc, 0)
        piece = send(piece, "weight")
        up_far = send(w_up, "weight")
        pieces = gather(piece)

        x = turn_t(turn_d(inputs[0]))
        x_own = x[:half_t]
        w_qkv, x = lax.optimization_barrier((w_qkv, x))
        wq, wv = w_qkv[:, 0], w_qkv[:, 2]
        wv_far = send(wv, "weight")
        wqo = jnp.concatenate([wq, w_out], axis=1)
        wqo_far = send(wqo, "weight")
        cot = turn_t(turn_d(cotangent[0]))[:half_t]
        out_b, gains, shifts = turn_d(out_biases), turn_d(norm_gains), turn_d(norm_shifts)
        x_lo, x_hi = x[:, :half_d], x[:, half_d:]

        k = (dot(x_lo, wk, NN) + dot(x_hi, wk_far, NN)).astype(BF)
        ks = gather(k)
        v = (dot(x_lo, wv, NN) + dot(x_hi, wv_far, NN) + head_bias[1]).astype(BF)
        vs = gather(v)
        q = dot(x_lo, wq, NN) + dot(x_hi, wqo_far[:, :cols], NN) + head_bias[0]
        q = q.astype(BF) * BF(HD**-0.5)
        qs = gather_few(q)

        part = (arr(half_t, width, F32), arr(half_t, width, BF))
        attended, lse, keep, sent = attend(q, wqo, wqo_far, ks, vs)
        sent, got = settle(keep, sent)
        mixed_one, normed_one, inverse_one, mixed_own = call(
            norm_one_kernel,
            (part[0], part[0], arr(half_t, 128, F32), part[1]),
            sent, got, x_own, out_b, gains, shifts,
        )
        mixed_got = send(mixed_own, "tensor")
        big = 2 * tokens * width * hidden
        pre_act, act, mixed_hi = call(
            up_kernel,
            (arr(tokens, hidden, F32), arr(tokens, hidden, BF), arr(tokens, half_d, BF)),
            mixed_own, mixed_got, w_up, up_far, up_bias.reshape(1, hidden),
            flops=big,
        )
        mixed_mate = send(mixed_hi, "weight")
        down_far, keep, sent = call(
            down_kernel,
            (arr(half_d, hidden, BF),) + part,
            ranks, act, w_down, *pieces,
            flops=big, scalars=1,
        )
        sent, got = settle(keep, sent)
        act_mate = send(act, "weight")
        pair, grad_two, sums_two = call(
            norm_two_kernel,
            (arr(tokens, width, BF), part[0], arr(3, width, F32)),
            sent, got, mixed_one, cot, out_b, gains, shifts,
        )
        pair_got = send(pair, "tensor")
        two_hi = jnp.concatenate([pair[:half_t, half_d:], pair_got[:half_t, half_d:]], axis=0)
        two_mate = send(two_hi, "weight")
        grad_pre, grad_up_b, keep, sent = call(
            back_kernel,
            (arr(tokens, hidden, BF), arr(1, hidden, F32)) + part,
            pair, pair_got, w_down, down_far, pre_act, w_up, up_far,
            flops=2 * big,
        )
        sent, got = settle(keep, sent)
        pre_mate = send(grad_pre, "weight")
        one_own, grad_one = call(
            norm_back_kernel,
            (arr(half_t + 32, width, BF), part[0]),
            sent, got, grad_two, normed_one, inverse_one, gains, sums_two,
        )
        one_got = send(one_own, "tensor")
        msg, bundle_own, vector = pack_message(
            flags, one_own, one_got, wqo, wqo_far, attended, lse, x, grad_up_b
        )
        msgs = gather(msg)
        bundle = send(bundle_own, "weight")
        bundle_got = send(bundle, "tensor")
        dq = query_grads(q, msg, attended, lse, ks, vs)
        dq_mate = send(dq, "weight")
        dkv = key_grads(k, v, qs, msgs)

        dkv_mate = send(dkv, "weight")
        keep, sent = call(
            input_kernel, part, dq, dkv, wqo, wk, wv, wqo_far, wk_far, wv_far,
            flops=6 * tokens * width * cols,
        )
        late = [sent] * 8

        def term(stack, b, low=0):
            stack = [(r, r.shape[0] if c is None else c) for r, c in stack]
            if not isinstance(b, list):
                b = [(b, sum(c for _, c in stack), 0, b.shape[1])]
            return stack, low, b, half_d

        mate = [(bundle, half_t), (bundle_got, half_t)]
        attended_mate = [(bundle, half_t, width, cols), (bundle, half_t, width + cols, cols)]

        grad_w_down = owned(
            [[term([(pair, half_t), (pair_got, half_t)], act), term([(two_mate, None)], act_mate)]],
            [dq] + late,
            mines,
        )
        grad_w_up = owned(
            [[
                term([(mixed_own, None), (mixed_got, None)], grad_pre),
                term([(mixed_mate, None)], pre_mate),
            ]],
            late,
            mines,
        )
        oq_grad = owned(
            [
                [
                    term([(one_own, half_t), (one_got, half_t)], attended),
                    term(mate, attended_mate),
                ],
                [term([(x, None)], dq), term(mate, dq_mate, low=half_d)],
            ],
            late,
            mines,
            (half_t, tokens, vector, bundle, dq, dq_mate),
        )
        sent, got = settle(keep, sent)
        grad_wkv = owned([[term([(x, None)], dkv), term(mate, dkv_mate, low=half_d)]], late, mines)
        grad_own = (grad_one + (sent.astype(F32) + got.astype(F32))).astype(BF)
        grad_got = send(grad_own, "tensor")
        grad_input = turn_d(turn_t(jnp.concatenate([grad_own, grad_got], axis=0)))
        pair, pair_got, _ = lax.optimization_barrier((pair, pair_got, grad_w_up[1]))
        layer_out = turn_d(turn_t(jnp.concatenate([pair[half_t:], pair_got[half_t:]], axis=0)))

        if half_d // nc % 128:
            rows = join_rows(bundle[half_t:, :width], 8) + vector
            sums = join_rows(dq[tokens:], 1) + join_rows(dq_mate[tokens:], 1)
            vector = jnp.concatenate(
                [rows[:7], jnp.concatenate([sums, rows[7:, cols:]], axis=1)], axis=0
            )
            bit = 1
            while bit < nc:
                vector = vector + send(vector, "ctx", bit)
                bit *= 2
        else:
            vector = oq_grad[2]
        block = half_d // nc
        down_grad, up_grad = call(
            add_kernel, (arr(block, hidden, F32),) * 2,
            *grad_w_down[:2], *grad_w_up[:2],
        )
        terms = [*oq_grad[:2], *grad_wkv[:2]]
        terms, layer_out, grad_input, down_grad, up_grad = lax.optimization_barrier(
            (terms, layer_out, grad_input, down_grad, up_grad)
        )
        out_grad, qkv_grad, head, up_row, bias, gain, shift = call(
            finish_kernel,
            (arr(block, cols, F32), jax.ShapeDtypeStruct((3, block, cols), F32), arr(2, cols, F32), arr(1, hidden, F32))
            + (arr(2, width, F32),) * 3,
            vector, *terms,
        )
        return (
            layer_out[None],
            grad_input[None],
            jnp.transpose(qkv_grad, (1, 0, 2)),
            out_grad,
            up_grad,
            down_grad,
            head,
            up_row[0],
            bias,
            gain,
            shift,
        )

    return local


def solution(mesh):
    return jax.shard_map(
        build(mesh.shape["weight"], mesh.shape["ctx"], mesh.shape["tensor"]),
        mesh=mesh,
        in_specs=(
            P("weight", "ctx", None),
            P("weight", None, "tensor"),
            P("weight", "tensor"),
            P("weight", "tensor"),
            P("weight", "tensor"),
            P(None, "tensor"),
            P("tensor"),
            P(),
            P(),
            P(),
            P("weight", "ctx", None),
        ),
        out_specs=(
            P("weight", "ctx", None),
            P("weight", "ctx", None),
            P(("weight", "ctx"), None, "tensor"),
            P(("weight", "ctx"), "tensor"),
            P(("weight", "ctx"), "tensor"),
            P(("weight", "ctx"), "tensor"),
            P(None, "tensor"),
            P("tensor"),
            P(),
            P(),
            P(),
        ),
        check_vma=False,
    )
```
